256 devices in a mesh: row: 8 (over z), col: 32 (over y, x, core).
Axes of the slice: x: 4, y: 4, z: 8, core: 2. Of those that a mesh axis runs over, the one named last changes fastest.
Arguments:
- factor: bfloat16 [32, 8, 8, 32, 128, 128], P(None, 'row', None, 'col'), may hold values from -0.046875 to 0.046875
- pattern: int32 [32, 8, 8, 32], P(None, 'row', None, 'col'), may hold values 0 or 1
- loads: float32 [8, 32, 128, 256], P(None, 'col'), may hold values from -6 to 6
- block_inverse: float32 [8, 32, 128, 128], P(None, 'col'), may hold values from -1 to 2, as said below
Outputs:
- solution: float32 [8, 32, 128, 256], P(None, 'col')
The draws below stay inside these ranges and needn't reach their ends.
Inputs may be any that keep to these rules, and one draw needn't show every extreme that they name: `block_inverse`: each block is lower triangular with diagonal entries between 0.5 and 1.5.
All inputs are finite; a program needn't handle non-finite values. No bound on the sum of `pattern` on one device may be relied on, other than what follows from the above.
Results may differ from the reference program's by a relative error of at most 0.0045.
Values may be sent and summed in bfloat16 or wider, within the bound.
No kernel may reach another device: no remote copies, remote signals or barrier semaphores. Data moves between devices by JAX's collectives and lax.ppermute only.
A program may use at most 128 MiB of HBM per device.

```python
import math
import jax
import jax.numpy as jnp
from jax import lax

BLOCK = 128
SCENARIOS = 256
LEVELS = 8
COL_BLOCKS = 1
LEVEL_BLOCKS = 32
BLOCKS = 256
N_ROW = 8
N_COL = 32


def draw_block_inverse(key, part):
    key_off, key_diag = jax.random.split(key)
    rows = lax.broadcasted_iota(jnp.int32, (BLOCK, BLOCK), 0)
    cols = lax.broadcasted_iota(jnp.int32, (BLOCK, BLOCK), 1)
    lower = (cols < rows).astype(jnp.float32)
    unit = (cols == rows).astype(jnp.float32)
    off_part = jax.random.normal(key_off, (BLOCKS, BLOCK, BLOCK), jnp.float32) * (0.5 / math.sqrt(BLOCK))
    off_part = jnp.clip(off_part, -0.9, 0.9)
    diag_part = jax.random.uniform(key_diag, (BLOCKS, 1, BLOCK), jnp.float32, 0.5, 1.5)
    blocks = off_part * lower + diag_part * unit
    return blocks.reshape(BLOCKS // N_COL, N_COL, BLOCK, BLOCK)


def set_ends(values, rng, least, top_value):
    place = [jax.random.randint(jax.random.fold_in(rng, axis), (), 0, length) for axis, length in enumerate(values.shape)]
    widest = values.shape.index(max(values.shape))
    beside = place[:widest] + [(place[widest] + 1) % values.shape[widest]] + place[widest + 1:]
    return values.at[tuple(place)].set(least).at[tuple(beside)].set(top_value)


def levels(rng, shape, cuts, least, largest):
    level, own = 1.0, jax.random.fold_in(rng, 6)
    for position, blocks in cuts:
        steps = jnp.exp(jax.random.uniform(jax.random.fold_in(own, position), (blocks,), jnp.float32, least / len(cuts), largest / len(cuts)))
        level = level * jnp.repeat(steps, shape[position] // blocks).reshape([-1 if axis == position else 1 for axis in range(len(shape))])
    return level


def scatter_about(rng, dims, scale, most, pieces=(), kind=jnp.bfloat16):
    values = scale * jax.random.normal(rng, dims, jnp.float32)
    if pieces:
        values = values * levels(rng, dims, pieces, -0.22, 0.18)
    return jnp.clip(values, -most, most).astype(kind)


def setup_inputs(seed: int = 0) -> dict:
    arg_keys = jax.random.split(jax.random.key(seed), 5)
    factor = scatter_about(arg_keys[0], (BLOCKS // N_ROW, N_ROW, BLOCKS // N_COL, N_COL, BLOCK, BLOCK), (BLOCKS * BLOCK // 2) ** -0.5, 0.046875, ((1, 8), (3, 32)))
    pattern = set_ends((jax.random.randint(arg_keys[1], (BLOCKS // N_ROW, N_ROW, BLOCKS // N_COL, N_COL), 0, 2) < 1).astype(jnp.int32), jax.random.fold_in(arg_keys[1], 1), 0, 1)
    loads = scatter_about(arg_keys[2], (BLOCKS // N_COL, N_COL, BLOCK, SCENARIOS), 1.0, 6.0, ((1, 32),), jnp.float32)
    block_inverse = draw_block_inverse(jax.random.fold_in(arg_keys[4], 71), 0)
    return dict(factor=factor, pattern=pattern, loads=loads, block_inverse=block_inverse)


def reference(factor, pattern, loads, block_inverse):
    masked = factor * pattern.astype(jnp.bfloat16)[:, :, :, :, None, None]
    per_row = LEVEL_BLOCKS // N_ROW
    rhs_all = loads.reshape(BLOCKS, BLOCK, SCENARIOS)
    inverse_all = block_inverse.reshape(BLOCKS, BLOCK, BLOCK)
    forward_vals = []
    forward_low = []
    for level_id in range(LEVELS):
        start = level_id * LEVEL_BLOCKS
        rhs_level = rhs_all[start:start + LEVEL_BLOCKS]
        if level_id > 0:
            panel = masked[level_id * per_row:(level_id + 1) * per_row, :, :level_id * COL_BLOCKS, :]
            panel = panel.reshape(LEVEL_BLOCKS, level_id * LEVEL_BLOCKS, BLOCK, BLOCK)
            earlier = jnp.concatenate(forward_low, axis=0)
            sums = jnp.einsum("ijpq,jqs->ips", panel.astype(jnp.float32), earlier.astype(jnp.float32))
            rhs_level = rhs_level - sums
        solved = jnp.einsum("ipq,iqs->ips", inverse_all[start:start + LEVEL_BLOCKS], rhs_level,
                            precision=lax.Precision.HIGHEST)
        forward_vals.append(solved)
        forward_low.append(lax.optimization_barrier(solved.astype(jnp.bfloat16)))
    solution_parts = [None] * LEVELS
    later = []
    for level_id in reversed(range(LEVELS)):
        start = level_id * LEVEL_BLOCKS
        resid = forward_vals[level_id]
        if level_id < LEVELS - 1:
            panel = masked[(level_id + 1) * per_row:, :, level_id * COL_BLOCKS:(level_id + 1) * COL_BLOCKS, :]
            panel = panel.reshape((LEVELS - 1 - level_id) * LEVEL_BLOCKS, LEVEL_BLOCKS, BLOCK, BLOCK)
            after = jnp.concatenate(later, axis=0)
            sums = jnp.einsum("ijpq,ips->jqs", panel.astype(jnp.float32), after.astype(jnp.float32))
            resid = resid - sums
        solved = jnp.einsum("jqp,jqs->jps", inverse_all[start:start + LEVEL_BLOCKS], resid,
                            precision=lax.Precision.HIGHEST)
        solution_parts[level_id] = solved
        later = [lax.optimization_barrier(solved.astype(jnp.bfloat16))] + later
    solution = jnp.concatenate(solution_parts, axis=0)
    return solution.reshape(BLOCKS // N_COL, N_COL, BLOCK, SCENARIOS)
```

```python
import jax
import jax.numpy as jnp
from jax import lax
from jax.sharding import Mesh
from jax.sharding import PartitionSpec as P

LEVELS = 8
NATIVE = 4
PER_ROW = 4
SUB = 8
BF16 = jnp.bfloat16
F32 = jnp.float32
HIGHEST = lax.Precision.HIGHEST
COL = ("grp", "sub")


def exchange(pieces, axis):
    return lax.all_to_all(pieces, axis, 0, 0, tiled=True)


def spread(piece, axis, count):
    return exchange(jnp.broadcast_to(piece[None], (count,) + piece.shape), axis)


def per_device(factor, pattern, loads, block_inverse):
    my_row = lax.axis_index("row")
    n_row = lax.axis_size("row")
    n_col = lax.axis_size("grp") * lax.axis_size("sub")
    scen = loads.shape[3]
    part = scen // n_row
    inverse = block_inverse[:, 0]
    loads_t = jnp.swapaxes(loads[:, 0], 1, 2)
    panels = [None]
    for t in range(1, LEVELS):
        rows = slice(t * PER_ROW, (t + 1) * PER_ROW)
        mask = pattern[rows, 0, :t, 0].astype(BF16)[:, :, None, None]
        panels.append(factor[rows, 0, :t, 0] * mask)
    full = [None] * LEVELS
    for t in range(NATIVE + 1, LEVELS):
        full[t] = lax.all_gather(panels[t], "row", axis=0)
    early = lax.all_gather(jnp.concatenate(panels[1 : NATIVE + 1], axis=1), "row", axis=0)
    at = 0
    for t in range(1, NATIVE + 1):
        full[t] = early[:, :, at : at + t]
        at += t

    def forward_solve(level, resid):
        return lax.dot_general(
            resid, inverse[level], (((1,), (1,)), ((), ())), precision=HIGHEST
        )

    def backward_solve(level, resid):
        return lax.dot_general(
            resid, inverse[level], (((1,), (0,)), ((), ())), precision=HIGHEST
        )

    solved = [forward_solve(0, loads_t[0])]
    low = [solved[0].astype(BF16)]
    for t in range(1, NATIVE + 1):
        sums = sum(
            jnp.einsum("sq,apq->asp", low[m], panels[t][:, m], preferred_element_type=F32)
            for m in range(t)
        )
        pieces = sums.astype(BF16).reshape(n_col, part, -1)
        total = jnp.sum(exchange(pieces, COL).astype(F32), axis=0).astype(BF16)
        total = exchange(spread(total, "row", n_row), "sub")
        total = total.reshape(scen, -1).astype(F32)
        solved.append(forward_solve(t, loads_t[t] - total))
        low.append(solved[t].astype(BF16))

    def own(value):
        return lax.dynamic_slice_in_dim(value, my_row * part, part, axis=0)

    solved = [own(v) for v in solved]
    low = [own(v) for v in low]
    for t in range(NATIVE + 1, LEVELS):
        sums = sum(
            jnp.einsum("sq,rapq->arsp", low[m], full[t][:, :, m], preferred_element_type=F32)
            for m in range(t)
        )
        pieces = sums.astype(BF16).reshape(n_col, part, -1)
        total = jnp.sum(exchange(pieces, COL).astype(F32), axis=0)
        solved.append(forward_solve(t, own(loads_t[t]) - total))
        low.append(solved[t].astype(BF16))

    out = [None] * LEVELS
    after = [None] * LEVELS
    out[LEVELS - 1] = backward_solve(LEVELS - 1, solved[LEVELS - 1])
    for j in reversed(range(LEVELS - 1)):
        spread_low = spread(out[j + 1].astype(BF16), COL, n_col)
        after[j + 1] = spread_low.reshape(PER_ROW, n_row, part, -1)
        total = sum(
            jnp.einsum(
                "arsp,rapq->sq", after[t], full[t][:, :, j], preferred_element_type=F32
            )
            for t in range(j + 1, LEVELS)
        )
        out[j] = backward_solve(j, solved[j] - total)
    both = spread(jnp.stack(out), "row", n_row)
    both = jnp.transpose(both, (1, 3, 0, 2)).reshape(LEVELS, 1, -1, scen)
    return both


def solution(mesh):
    n_col = mesh.shape["col"]
    n_row = mesh.shape["row"]
    split = Mesh(
        mesh.devices.reshape(n_row, n_col // SUB, SUB), ("row", "grp", "sub")
    )
    in_specs = (
        P(None, "row", None, COL, None, None),
        P(None, "row", None, COL),
        P(None, COL, None, None),
        P(None, COL, None, None),
    )
    return jax.shard_map(
        per_device, mesh=split, in_specs=in_specs, out_specs=P(None, COL, None, None), check_vma=False
    )
```

```python
import functools

import jax
import jax.numpy as jnp
from jax import lax
from jax.experimental import pallas as pl
from jax.experimental.pallas import tpu as pltpu
from jax.sharding import Mesh
from jax.sharding import PartitionSpec as P

LEVELS = 8
NATIVE = 3
PER_ROW = 4
SUB = 8
BF16 = jnp.bfloat16
F32 = jnp.float32
HIGHEST = lax.Precision.HIGHEST
COL = ("grp", "sub")
ALL = ("row", "grp", "sub")
CHUNKS = ((6, 5, 4, 3, 2), (1, 0))


def exchange(pieces, axis):
    return lax.all_to_all(pieces, axis, 0, 0, tiled=True)


def spread(piece, axis, count):
    return exchange(jnp.broadcast_to(piece[None], (count,) + piece.shape), axis)


def times_column(x_ref, g_ref, row):
    x = jnp.concatenate([x_ref[a, row] for a in range(PER_ROW)], axis=1)
    g = g_ref[0].reshape(-1, g_ref.shape[-1])
    return jnp.dot(x, g, preferred_element_type=F32)


def far_kernel(count, *refs):
    x_refs, g_refs, out_ref = refs[:count], refs[count : 2 * count], refs[2 * count]
    row = pl.program_id(0)

    @pl.when(row == 0)
    def _():
        out_ref[...] = jnp.zeros_like(out_ref)

    out_ref[...] += sum(times_column(x, g, row) for x, g in zip(x_refs, g_refs))


def near_kernel(x_ref, g_ref, rest_ref, inverse_ref, out_ref, low_ref, acc_ref):
    row = pl.program_id(0)

    @pl.when(row == 0)
    def _():
        acc_ref[...] = rest_ref[...]

    acc_ref[...] -= times_column(x_ref, g_ref, row)

    @pl.when(row == pl.num_programs(0) - 1)
    def _():
        solved = jnp.dot(
            acc_ref[...], inverse_ref[...], precision=HIGHEST, preferred_element_type=F32
        )
        out_ref[...] = solved
        low_ref[...] = jnp.broadcast_to(solved.astype(BF16)[None], low_ref.shape)


def whole(shape):
    return pl.BlockSpec(shape, lambda r: (0,) * len(shape))


def column_spec(first, block):
    return pl.BlockSpec((1, PER_ROW, block, block), lambda r: (r, first, 0, 0))


def far_sums(xs, packed, firsts):
    n_row, part, block = xs[0].shape[1:]
    return pl.pallas_call(
        functools.partial(far_kernel, len(xs)),
        grid=(n_row,),
        in_specs=[whole(x.shape) for x in xs] + [column_spec(f, block) for f in firsts],
        out_specs=whole((part, block)),
        out_shape=jax.ShapeDtypeStruct((part, block), F32),
        cost_estimate=pl.CostEstimate(
            flops=2 * len(xs) * n_row * PER_ROW * part * block * block,
            bytes_accessed=2 * len(xs) * n_row * PER_ROW * block * block,
            transcendentals=0,
        ),
        name="far_sums",
    )(*xs, *([packed] * len(xs)))


def near_solve(x, packed, first, rest, inverse, n_col):
    n_row, part, block = x.shape[1:]
    return pl.pallas_call(
        near_kernel,
        grid=(n_row,),
        in_specs=[
            whole(x.shape),
            column_spec(first, block),
            whole(rest.shape),
            whole(inverse.shape),
        ],
        out_specs=[whole((part, block)), whole((n_col, part, block))],
        out_shape=[
            jax.ShapeDtypeStruct((part, block), F32),
            jax.ShapeDtypeStruct((n_col, part, block), BF16),
        ],
        scratch_shapes=[pltpu.VMEM((part, block), F32)],
        cost_estimate=pl.CostEstimate(
            flops=2 * n_row * PER_ROW * part * block * block,
            bytes_accessed=2 * n_row * PER_ROW * block * block,
            transcendentals=0,
        ),
        name="near_solve",
    )(x, packed, rest, inverse)


def per_device(factor, pattern, loads, block_inverse):
    my_row = lax.axis_index("row")
    n_row = lax.axis_size("row")
    n_grp = lax.axis_size("grp")
    n_sub = lax.axis_size("sub")
    n_col = n_grp * n_sub
    scen = loads.shape[3]
    block = loads.shape[2]
    part = scen // n_row
    inverse = block_inverse[:, 0]
    loads_t = jnp.swapaxes(loads[:, 0], 1, 2)

    columns = []
    for j in range(LEVELS - 1):
        rows = slice((j + 1) * PER_ROW, LEVELS * PER_ROW)
        mask = pattern[rows, 0, j, 0].astype(BF16)[:, None, None]
        columns.append(factor[rows, 0, j, 0] * mask)
    gathered, where = [None] * LEVELS, [None] * LEVELS
    for chunk in CHUNKS:
        packed = jnp.concatenate([columns[j] for j in chunk], axis=0)
        packed = lax.all_gather(packed, "row", axis=0)
        at = 0
        for j in chunk:
            size = columns[j].shape[0]
            gathered[j], where[j] = packed, at // PER_ROW
            at += size

    def local(t, m):
        return columns[m][(t - m - 1) * PER_ROW : (t - m) * PER_ROW]

    def split(t, m):
        at = (where[m] + t - m - 1) * PER_ROW
        return gathered[m][:, at : at + PER_ROW]

    def forward_solve(level, resid):
        return lax.dot_general(
            resid, inverse[level], (((1,), (1,)), ((), ())), precision=HIGHEST
        )

    def backward_solve(level, resid):
        return lax.dot_general(
            resid, inverse[level], (((1,), (0,)), ((), ())), precision=HIGHEST
        )

    def local_sums(t, count):
        return sum(
            jnp.einsum("sq,apq->asp", low[m], local(t, m), preferred_element_type=F32)
            for m in range(count)
        ).astype(BF16)

    solved = [forward_solve(0, loads_t[0])]
    low = [solved[0].astype(BF16)]
    for t in range(1, NATIVE + 1):
        pieces = local_sums(t, t).reshape(n_col, part, block)
        total = jnp.sum(exchange(pieces, COL).astype(F32), axis=0).astype(BF16)
        total = exchange(spread(total, "row", n_row), "sub")
        total = total.reshape(scen, block).astype(F32)
        solved.append(forward_solve(t, loads_t[t] - total))
        low.append(solved[t].astype(BF16))

    pieces = jnp.stack(
        [local_sums(t, NATIVE + 1).reshape(n_col, part, block) for t in range(NATIVE + 1, LEVELS)],
        axis=1,
    )
    total = jnp.sum(exchange(pieces, COL).astype(F32), axis=0).astype(BF16)
    turn = [
        ((r * n_grp + g) * n_sub + k, (k * n_grp + g) * n_sub + r)
        for r in range(n_row)
        for g in range(n_grp)
        for k in range(n_sub)
    ]
    early = lax.ppermute(total, ALL, turn).astype(F32)

    def own(value):
        return lax.dynamic_slice_in_dim(value, my_row * part, part, axis=0)

    solved = [own(v) for v in solved]
    low = low + [None] * (LEVELS - NATIVE - 1)
    for t in range(NATIVE + 1, LEVELS):
        total = early[t - NATIVE - 1]
        if t > NATIVE + 1:
            sums = sum(
                jnp.einsum("sq,rapq->arsp", low[m], split(t, m), preferred_element_type=F32)
                for m in range(NATIVE + 1, t)
            )
            pieces = sums.astype(BF16).reshape(n_col, part, block)
            total = total + jnp.sum(exchange(pieces, COL).astype(F32), axis=0)
        solved.append(forward_solve(t, own(loads_t[t]) - total))
        low[t] = solved[t].astype(BF16)

    out = [None] * LEVELS
    out[LEVELS - 1] = backward_solve(LEVELS - 1, solved[LEVELS - 1])
    wide = jnp.broadcast_to(out[LEVELS - 1].astype(BF16)[None], (n_col, part, block))
    later = []
    for j in reversed(range(LEVELS - 1)):
        rest = solved[j]
        if later:
            rest = rest - far_sums(
                [x for _, x in later],
                gathered[j],
                [where[j] + t - j - 1 for t, _ in later],
            )
        near = exchange(wide, COL).reshape(PER_ROW, n_row, part, block)
        out[j], wide = near_solve(near, gathered[j], where[j], rest, inverse[j], n_col)
        later.append((j + 1, near))

    both = spread(jnp.stack(out).astype(BF16), "row", n_row)
    return jnp.transpose(both, (1, 3, 0, 2)).reshape(LEVELS, 1, block, scen).astype(F32)


def solution(mesh):
    n_col = mesh.shape["col"]
    n_row = mesh.shape["row"]
    devices = mesh.devices.reshape(n_row, n_col // SUB, SUB)
    in_specs = (
        P(None, "row", None, COL, None, None),
        P(None, "row", None, COL),
        P(None, COL, None, None),
        P(None, COL, None, None),
    )
    return jax.shard_map(
        per_device,
        mesh=Mesh(devices, ALL),
        in_specs=in_specs,
        out_specs=P(None, COL, None, None),
        check_vma=False,
    )
```

```python
import functools

import jax
import jax.numpy as jnp
from jax import lax
from jax.experimental import pallas as pl
from jax.experimental.pallas import tpu as pltpu
from jax.sharding import Mesh
from jax.sharding import PartitionSpec as P

LEVELS = 8
NATIVE = 2
FAR_STEPS = 2
PER_ROW = 4
SUB = 8
BF16 = jnp.bfloat16
F32 = jnp.float32
HIGHEST = lax.Precision.HIGHEST
COL = ("grp", "sub")
ALL = ("row", "grp", "sub")
CHUNKS = ((6, 5, 4, 3), (2, 1), (0,))


def exchange(pieces, axis):
    return lax.all_to_all(pieces, axis, 0, 0, tiled=True)


def spread(piece, axis, count):
    return exchange(jnp.broadcast_to(piece[None], (count,) + piece.shape), axis)


def times_column(x_ref, g_ref, rows):
    x = jnp.concatenate([x_ref[a, r] for r in rows for a in range(PER_ROW)], axis=1)
    g = g_ref[...].reshape(-1, g_ref.shape[-1])
    return jnp.dot(x, g, preferred_element_type=F32)


def far_kernel(count, *refs):
    y_ref, x_refs, g_refs, out_ref = refs[0], refs[1 : count + 1], refs[count + 1 : -1], refs[-1]
    n_row = x_refs[0].shape[1]
    step = n_row // FAR_STEPS
    for s in range(FAR_STEPS):

        @pl.when(pl.program_id(0) == s)
        def _():
            rows = range(s * step, (s + 1) * step)
            got = sum(times_column(x, g, rows) for x, g in zip(x_refs, g_refs))
            out_ref[...] = (y_ref[...] if s == 0 else out_ref[...]) - got


def near_kernel(x_ref, g_ref, rest_ref, inverse_ref, out_ref, low_ref):
    got = times_column(x_ref, g_ref, range(x_ref.shape[1]))
    solved = jnp.dot(
        rest_ref[...] - got, inverse_ref[...], precision=HIGHEST, preferred_element_type=F32
    )
    out_ref[...] = solved
    low_ref[...] = jnp.broadcast_to(solved.astype(BF16)[None], low_ref.shape)


def whole(shape):
    return pl.BlockSpec(shape, lambda s: (0,) * len(shape))


def column_spec(rows, first, block):
    return pl.BlockSpec((rows, PER_ROW, block, block), lambda s: (s, first, 0, 0))


def far_rest(y, xs, packed, firsts):
    n_row, part, block = xs[0].shape[1:]
    step = n_row // FAR_STEPS
    return pl.pallas_call(
        functools.partial(far_kernel, len(xs)),
        grid=(FAR_STEPS,),
        in_specs=[whole(y.shape)]
        + [whole(x.shape) for x in xs]
        + [column_spec(step, f, block) for f in firsts],
        out_specs=whole((part, block)),
        out_shape=jax.ShapeDtypeStruct((part, block), F32),
        cost_estimate=pl.CostEstimate(
            flops=2 * len(xs) * n_row * PER_ROW * part * block * block,
            bytes_accessed=2 * len(xs) * n_row * PER_ROW * block * block,
            transcendentals=0,
        ),
        name="far_rest",
    )(y, *xs, *([packed] * len(xs)))


def near_solve(x, packed, first, rest, inverse, n_col):
    n_row, part, block = x.shape[1:]
    return pl.pallas_call(
        near_kernel,
        grid=(1,),
        in_specs=[
            whole(x.shape),
            column_spec(n_row, first, block),
            whole(rest.shape),
            whole(inverse.shape),
        ],
        out_specs=[whole((part, block)), whole((n_col, part, block))],
        out_shape=[
            jax.ShapeDtypeStruct((part, block), F32),
            jax.ShapeDtypeStruct((n_col, part, block), BF16),
        ],
        cost_estimate=pl.CostEstimate(
            flops=2 * n_row * PER_ROW * part * block * block,
            bytes_accessed=2 * n_row * PER_ROW * block * block,
            transcendentals=0,
        ),
        name="near_solve",
    )(x, packed, rest, inverse)


def per_device(factor, pattern, loads, block_inverse):
    my_row = lax.axis_index("row")
    n_row = lax.axis_size("row")
    n_grp = lax.axis_size("grp")
    n_sub = lax.axis_size("sub")
    n_col = n_grp * n_sub
    scen = loads.shape[3]
    block = loads.shape[2]
    part = scen // n_row
    inverse = block_inverse[:, 0]
    loads_t = jnp.swapaxes(loads[:, 0], 1, 2)

    def forward_solve(level, resid):
        return lax.dot_general(
            resid, inverse[level], (((1,), (1,)), ((), ())), precision=HIGHEST
        )

    def backward_solve(level, resid):
        return lax.dot_general(
            resid, inverse[level], (((1,), (0,)), ((), ())), precision=HIGHEST
        )

    solved = [forward_solve(0, loads_t[0])]
    low = [solved[0].astype(BF16)]

    flags = pattern[:, 0, :, 0].astype(BF16)
    flags_after, low[0] = lax.optimization_barrier((flags, low[0]))

    def column(j, flags):
        rows = slice((j + 1) * PER_ROW, LEVELS * PER_ROW)
        return factor[rows, 0, j, 0] * flags[rows, j][:, None, None]

    columns = [column(j, flags) for j in range(LEVELS - 1)]
    gathered, where = [None] * LEVELS, [None] * LEVELS
    for chunk in CHUNKS:
        use = flags if chunk is CHUNKS[0] else flags_after
        packed = jnp.concatenate([column(j, use) for j in chunk], axis=0)
        packed = lax.all_gather(packed, "row", axis=0)
        at = 0
        for j in chunk:
            size = columns[j].shape[0]
            gathered[j], where[j] = packed, at // PER_ROW
            at += size

    def local(t, m):
        return columns[m][(t - m - 1) * PER_ROW : (t - m) * PER_ROW]

    def split(t, m):
        at = (where[m] + t - m - 1) * PER_ROW
        return gathered[m][:, at : at + PER_ROW]

    def local_sums(t, count):
        return sum(
            jnp.einsum("sq,apq->asp", low[m], local(t, m), preferred_element_type=F32)
            for m in range(count)
        ).astype(BF16)

    for t in range(1, NATIVE + 1):
        pieces = local_sums(t, t).reshape(n_col, part, block)
        total = jnp.sum(exchange(pieces, COL).astype(F32), axis=0).astype(BF16)
        total = exchange(spread(total, "row", n_row), "sub")
        total = total.reshape(scen, block).astype(F32)
        solved.append(forward_solve(t, loads_t[t] - total))
        low.append(solved[t].astype(BF16))

    pieces = jnp.stack(
        [local_sums(t, NATIVE + 1).reshape(n_col, part, block) for t in range(NATIVE + 1, LEVELS)],
        axis=1,
    )
    total = jnp.sum(exchange(pieces, COL).astype(F32), axis=0).astype(BF16)
    turn = [
        ((r * n_grp + g) * n_sub + k, (k * n_grp + g) * n_sub + r)
        for r in range(n_row)
        for g in range(n_grp)
        for k in range(n_sub)
    ]
    early = lax.ppermute(total, ALL, turn).astype(F32)

    def own(value):
        return lax.dynamic_slice_in_dim(value, my_row * part, part, axis=0)

    solved = [own(v) for v in solved]
    low = low + [None] * (LEVELS - NATIVE - 1)
    for t in range(NATIVE + 1, LEVELS):
        total = early[t - NATIVE - 1]
        if t > NATIVE + 1:
            sums = sum(
                jnp.einsum("sq,rapq->arsp", low[m], split(t, m), preferred_element_type=F32)
                for m in range(NATIVE + 1, t)
            )
            pieces = sums.astype(BF16).reshape(n_col, part, block)
            total = total + jnp.sum(exchange(pieces, COL).astype(F32), axis=0)
        solved.append(forward_solve(t, own(loads_t[t]) - total))
        low[t] = solved[t].astype(BF16)

    out = [None] * LEVELS
    out[LEVELS - 1] = backward_solve(LEVELS - 1, solved[LEVELS - 1])
    wide = jnp.broadcast_to(out[LEVELS - 1].astype(BF16)[None], (n_col, part, block))
    later = []
    for j in reversed(range(LEVELS - 1)):
        rest = solved[j]
        if later:
            rest = far_rest(
                rest,
                [x for _, x in later],
                gathered[j],
                [where[j] + t - j - 1 for t, _ in later],
            )
        near = exchange(wide, COL).reshape(PER_ROW, n_row, part, block)
        out[j], wide = near_solve(near, gathered[j], where[j], rest, inverse[j], n_col)
        later.append((j + 1, near))

    both = spread(jnp.stack(out).astype(BF16), "row", n_row)
    return jnp.transpose(both, (1, 3, 0, 2)).reshape(LEVELS, 1, block, scen).astype(F32)


def solution(mesh):
    n_col = mesh.shape["col"]
    n_row = mesh.shape["row"]
    devices = mesh.devices.reshape(n_row, n_col // SUB, SUB)
    in_specs = (
        P(None, "row", None, COL, None, None),
        P(None, "row", None, COL),
        P(None, COL, None, None),
        P(None, COL, None, None),
    )
    return jax.shard_map(
        per_device,
        mesh=Mesh(devices, ALL),
        in_specs=in_specs,
        out_specs=P(None, COL, None, None),
        check_vma=False,
    )
```

```python
import functools

import jax
import jax.numpy as jnp
from jax import lax
from jax.experimental import pallas as pl
from jax.experimental.pallas import tpu as pltpu
from jax.sharding import Mesh
from jax.sharding import PartitionSpec as P

LEVELS = 8
NATIVE = 2
FAR_STEPS = 2
PER_ROW = 4
SUB = 8
BF16 = jnp.bfloat16
F32 = jnp.float32
HIGHEST = lax.Precision.HIGHEST
COL = ("grp", "sub")
ALL = ("row", "grp", "sub")
CHUNKS = (
    ((6, 7, 8), (5, 6, 8), (4, 5, 8), (3, 4, 8)),
    ((2, 3, 5), (1, 2, 5)),
    ((0, 1, 5),),
)
CROSS_FROM, CROSS_TO = 5, 3
CROSS_STEPS = 4


def exchange(pieces, axis):
    return lax.all_to_all(pieces, axis, 0, 0, tiled=True)


def spread(piece, axis, count):
    return exchange(jnp.broadcast_to(piece[None], (count,) + piece.shape), axis)


def times_column(x_ref, g_ref, rows):
    x = jnp.concatenate([x_ref[a, r] for r in rows for a in range(PER_ROW)], axis=1)
    g = g_ref[...].reshape(-1, g_ref.shape[-1])
    return jnp.dot(x, g, preferred_element_type=F32)


def far_kernel(count, *refs):
    y_ref, x_refs, g_refs, out_ref = refs[0], refs[1 : count + 1], refs[count + 1 : -1], refs[-1]
    n_row = x_refs[0].shape[1]
    step = n_row // FAR_STEPS
    for s in range(FAR_STEPS):

        @pl.when(pl.program_id(0) == s)
        def _():
            rows = range(s * step, (s + 1) * step)
            got = sum(times_column(x, g, rows) for x, g in zip(x_refs, g_refs))
            out_ref[...] = (y_ref[...] if s == 0 else out_ref[...]) - got


def cross_kernel(x_ref, g_ref, out_ref):
    x = jnp.concatenate([x_ref[a] for a in range(x_ref.shape[0])], axis=1)
    for k in range(g_ref.shape[0]):
        for j in range(g_ref.shape[1]):
            g = g_ref[k, j].reshape(-1, g_ref.shape[-1])
            out_ref[k, j] = jnp.dot(x, g, preferred_element_type=F32).astype(BF16)


def cross_sums(x, g):
    n_sub, count, depth, block, _ = g.shape
    part = x.shape[1]
    step = n_sub // CROSS_STEPS
    return pl.pallas_call(
        cross_kernel,
        grid=(CROSS_STEPS,),
        in_specs=[
            whole(x.shape),
            pl.BlockSpec((step, count, depth, block, block), lambda s: (s, 0, 0, 0, 0)),
        ],
        out_specs=pl.BlockSpec((step, count, part, block), lambda s: (s, 0, 0, 0)),
        out_shape=jax.ShapeDtypeStruct((n_sub, count, part, block), BF16),
        cost_estimate=pl.CostEstimate(
            flops=2 * n_sub * count * depth * part * block * block,
            bytes_accessed=2 * n_sub * count * depth * block * block,
            transcendentals=0,
        ),
        name="cross_sums",
    )(x, g)


def near_kernel(x_ref, g_ref, rest_ref, inverse_ref, out_ref, low_ref):
    got = times_column(x_ref, g_ref, range(x_ref.shape[1]))
    solved = jnp.dot(
        rest_ref[...] - got, inverse_ref[...], precision=HIGHEST, preferred_element_type=F32
    )
    out_ref[...] = solved
    low_ref[...] = jnp.broadcast_to(solved.astype(BF16)[None], low_ref.shape)


def whole(shape):
    return pl.BlockSpec(shape, lambda s: (0,) * len(shape))


def column_spec(rows, first, block):
    return pl.BlockSpec((rows, PER_ROW, block, block), lambda s: (s, first, 0, 0))


def far_rest(y, xs, packed, firsts):
    n_row, part, block = xs[0].shape[1:]
    step = n_row // FAR_STEPS
    return pl.pallas_call(
        functools.partial(far_kernel, len(xs)),
        grid=(FAR_STEPS,),
        in_specs=[whole(y.shape)]
        + [whole(x.shape) for x in xs]
        + [column_spec(step, f, block) for f in firsts],
        out_specs=whole((part, block)),
        out_shape=jax.ShapeDtypeStruct((part, block), F32),
        cost_estimate=pl.CostEstimate(
            flops=2 * len(xs) * n_row * PER_ROW * part * block * block,
            bytes_accessed=2 * len(xs) * n_row * PER_ROW * block * block,
            transcendentals=0,
        ),
        name="far_rest",
    )(y, *xs, *([packed] * len(xs)))


def near_solve(x, packed, first, rest, inverse, n_col):
    n_row, part, block = x.shape[1:]
    return pl.pallas_call(
        near_kernel,
        grid=(1,),
        in_specs=[
            whole(x.shape),
            column_spec(n_row, first, block),
            whole(rest.shape),
            whole(inverse.shape),
        ],
        out_specs=[whole((part, block)), whole((n_col, part, block))],
        out_shape=[
            jax.ShapeDtypeStruct((part, block), F32),
            jax.ShapeDtypeStruct((n_col, part, block), BF16),
        ],
        cost_estimate=pl.CostEstimate(
            flops=2 * n_row * PER_ROW * part * block * block,
            bytes_accessed=2 * n_row * PER_ROW * block * block,
            transcendentals=0,
        ),
        name="near_solve",
    )(x, packed, rest, inverse)


def per_device(factor, pattern, loads, block_inverse):
    my_row = lax.axis_index("row")
    n_row = lax.axis_size("row")
    n_grp = lax.axis_size("grp")
    n_sub = lax.axis_size("sub")
    n_col = n_grp * n_sub
    scen = loads.shape[3]
    block = loads.shape[2]
    part = scen // n_row
    inverse = block_inverse[:, 0]
    loads_t = jnp.swapaxes(loads[:, 0], 1, 2)

    def forward_solve(level, resid):
        return lax.dot_general(
            resid, inverse[level], (((1,), (1,)), ((), ())), precision=HIGHEST
        )

    def backward_solve(level, resid):
        return lax.dot_general(
            resid, inverse[level], (((1,), (0,)), ((), ())), precision=HIGHEST
        )

    solved = [forward_solve(0, loads_t[0])]
    low = [solved[0].astype(BF16)]

    flags = pattern[:, 0, :, 0].astype(BF16)
    flags_after, low[0] = lax.optimization_barrier((flags, low[0]))

    def column(j, first, end, flags):
        rows = slice(first * PER_ROW, end * PER_ROW)
        return factor[rows, 0, j, 0] * flags[rows, j][:, None, None]

    columns = [column(j, j + 1, LEVELS, flags) for j in range(LEVELS - 1)]

    def crossing():
        blocks = [column(j, CROSS_FROM, LEVELS, flags_after) for j in range(CROSS_TO)]
        return lax.all_gather(jnp.stack(blocks), "sub", axis=0)

    place = {}
    for at_chunk, chunk in enumerate(CHUNKS):
        use = flags_after if at_chunk else flags
        packed = jnp.concatenate([column(j, a, b, use) for j, a, b in chunk], axis=0)
        packed = lax.all_gather(packed, "row", axis=0)
        at = 0
        for j, a, b in chunk:
            for t in range(a, b):
                place[t, j] = packed, at
                at += 1
        if at_chunk == 0:
            crossed = crossing()

    def local(t, m):
        return columns[m][(t - m - 1) * PER_ROW : (t - m) * PER_ROW]

    def split(t, m):
        packed, at = place[t, m]
        return packed[:, at * PER_ROW : (at + 1) * PER_ROW]

    def local_sums(t, count):
        return sum(
            jnp.einsum("sq,apq->asp", low[m], local(t, m), preferred_element_type=F32)
            for m in range(count)
        ).astype(BF16)

    for t in range(1, NATIVE + 1):
        pieces = local_sums(t, t).reshape(n_col, part, block)
        total = jnp.sum(exchange(pieces, COL).astype(F32), axis=0).astype(BF16)
        total = exchange(spread(total, "row", n_row), "sub")
        total = total.reshape(scen, block).astype(F32)
        solved.append(forward_solve(t, loads_t[t] - total))
        low.append(solved[t].astype(BF16))

    pieces = jnp.stack(
        [local_sums(t, NATIVE + 1).reshape(n_col, part, block) for t in range(NATIVE + 1, LEVELS)],
        axis=1,
    )
    total = jnp.sum(exchange(pieces, COL).astype(F32), axis=0).astype(BF16)
    turn = [
        ((r * n_grp + g) * n_sub + k, (k * n_grp + g) * n_sub + r)
        for r in range(n_row)
        for g in range(n_grp)
        for k in range(n_sub)
    ]
    early = lax.ppermute(total, ALL, turn).astype(F32)

    def own(value):
        return lax.dynamic_slice_in_dim(value, my_row * part, part, axis=0)

    solved = [own(v) for v in solved]
    low = low + [None] * (LEVELS - NATIVE - 1)
    for t in range(NATIVE + 1, LEVELS):
        total = early[t - NATIVE - 1]
        if t > NATIVE + 1:
            sums = sum(
                jnp.einsum("sq,rapq->arsp", low[m], split(t, m), preferred_element_type=F32)
                for m in range(NATIVE + 1, t)
            )
            pieces = sums.astype(BF16).reshape(n_col, part, block)
            total = total + jnp.sum(exchange(pieces, COL).astype(F32), axis=0)
        solved.append(forward_solve(t, own(loads_t[t]) - total))
        low[t] = solved[t].astype(BF16)

    out = [None] * LEVELS
    out[LEVELS - 1] = backward_solve(LEVELS - 1, solved[LEVELS - 1])
    wide = jnp.broadcast_to(out[LEVELS - 1].astype(BF16)[None], (n_col, part, block))
    later = []
    for j in reversed(range(LEVELS - 1)):
        rest = solved[j]
        if j < CROSS_TO:
            rest = rest - cross[j]
        far = [(t, x) for t, x in later if (t, j) in place]
        if far:
            rest = far_rest(
                rest, [x for _, x in far], place[far[0][0], j][0], [place[t, j][1] for t, _ in far]
            )
        near = exchange(wide, COL).reshape(PER_ROW, n_row, part, block)
        packed, at = place[j + 1, j]
        out[j], wide = near_solve(near, packed, at, rest, inverse[j], n_col)
        later.append((j + 1, near))
        if j + 1 == CROSS_FROM:
            mine = [
                lax.dynamic_index_in_dim(x, lax.axis_index("sub"), axis=1, keepdims=False)
                for _, x in reversed(later)
            ]
            mine, wide = lax.optimization_barrier((jnp.concatenate(mine, axis=0), wide))
            mine = lax.ppermute(mine, ALL, turn)
            cross = exchange(cross_sums(mine, crossed), "row")
            cross = lax.ppermute(jnp.sum(cross.astype(F32), axis=0), ALL, turn)

    both = spread(jnp.stack(out).astype(BF16), "row", n_row)
    return jnp.transpose(both, (1, 3, 0, 2)).reshape(LEVELS, 1, block, scen).astype(F32)


def solution(mesh):
    n_col = mesh.shape["col"]
    n_row = mesh.shape["row"]
    devices = mesh.devices.reshape(n_row, n_col // SUB, SUB)
    in_specs = (
        P(None, "row", None, COL, None, None),
        P(None, "row", None, COL),
        P(None, COL, None, None),
        P(None, COL, None, None),
    )
    return jax.shard_map(
        per_device,
        mesh=Mesh(devices, ALL),
        in_specs=in_specs,
        out_specs=P(None, COL, None, None),
        check_vma=False,
    )
```

```python
import functools

import jax
import jax.numpy as jnp
from jax import lax
from jax.experimental import pallas as pl
from jax.experimental.pallas import tpu as pltpu
from jax.sharding import Mesh
from jax.sharding import PartitionSpec as P

LEVELS = 8
NATIVE = 2
FAR_STEPS = 2
PER_ROW = 4
SUB = 8
BF16 = jnp.bfloat16
F32 = jnp.float32
HIGHEST = lax.Precision.HIGHEST
COL = ("grp", "sub")
ALL = ("row", "grp", "sub")
CHUNKS = (
    ((6, 7, 8), (5, 6, 8), (4, 5, 8), (3, 4, 8)),
    ((2, 3, 5), (1, 2, 5)),
    ((0, 1, 5),),
)
CROSS_FROM, CROSS_TO = 5, 3
CROSS_STEPS = 4


def exchange(pieces, axis):
    return lax.all_to_all(pieces, axis, 0, 0, tiled=True)


def spread(piece, axis, count):
    return exchange(jnp.broadcast_to(piece[None], (count,) + piece.shape), axis)


def times_column(x_ref, g_ref, rows):
    x = jnp.concatenate([x_ref[a, r] for r in rows for a in range(PER_ROW)], axis=1)
    g = g_ref[...].reshape(-1, g_ref.shape[-1])
    return jnp.dot(x, g, preferred_element_type=F32)


def far_kernel(count, *refs):
    y_ref, x_refs, g_refs, out_ref = refs[0], refs[1 : count + 1], refs[count + 1 : -1], refs[-1]
    n_row = x_refs[0].shape[1]
    step = n_row // FAR_STEPS
    for s in range(FAR_STEPS):

        @pl.when(pl.program_id(0) == s)
        def _():
            rows = range(s * step, (s + 1) * step)
            got = sum(times_column(x, g, rows) for x, g in zip(x_refs, g_refs))
            out_ref[...] = (y_ref[...] if s == 0 else out_ref[...]) - got


def cross_kernel(x_ref, g_ref, out_ref):
    x = jnp.concatenate([x_ref[a] for a in range(x_ref.shape[0])], axis=1)
    for k in range(g_ref.shape[0]):
        for j in range(g_ref.shape[1]):
            g = g_ref[k, j].reshape(-1, g_ref.shape[-1])
            out_ref[k, j] = jnp.dot(x, g, preferred_element_type=F32).astype(BF16)


def cross_sums(x, g):
    n_sub, count, depth, block, _ = g.shape
    part = x.shape[1]
    step = n_sub // CROSS_STEPS
    return pl.pallas_call(
        cross_kernel,
        grid=(CROSS_STEPS,),
        in_specs=[
            whole(x.shape),
            pl.BlockSpec((step, count, depth, block, block), lambda s: (s, 0, 0, 0, 0)),
        ],
        out_specs=pl.BlockSpec((step, count, part, block), lambda s: (s, 0, 0, 0)),
        out_shape=jax.ShapeDtypeStruct((n_sub, count, part, block), BF16),
        cost_estimate=pl.CostEstimate(
            flops=2 * n_sub * count * depth * part * block * block,
            bytes_accessed=2 * n_sub * count * depth * block * block,
            transcendentals=0,
        ),
        name="cross_sums",
    )(x, g)


def times_row(y, g):
    g = g.reshape(-1, g.shape[-1])
    return lax.dot_general(y, g, (((1,), (1,)), ((), ())), preferred_element_type=F32)


def ahead_kernel(count, *refs):
    y_refs, g_refs, out_ref = refs[:count], refs[count:-1], refs[-1]
    block = out_ref.shape[-1]
    for r in range(out_ref.shape[0]):
        got = sum(times_row(y[...], g[r]) for y, g in zip(y_refs, g_refs))
        for a in range(PER_ROW):
            out_ref[r, a] = got[:, a * block : (a + 1) * block]


def ahead_sums(ys, packed, firsts, n_row):
    part, block = ys[0].shape
    step = n_row // FAR_STEPS
    return pl.pallas_call(
        functools.partial(ahead_kernel, len(ys)),
        grid=(FAR_STEPS,),
        in_specs=[whole(y.shape) for y in ys] + [column_spec(step, f, block) for f in firsts],
        out_specs=pl.BlockSpec((step, PER_ROW, part, block), lambda s: (s, 0, 0, 0)),
        out_shape=jax.ShapeDtypeStruct((n_row, PER_ROW, part, block), F32),
        cost_estimate=pl.CostEstimate(
            flops=2 * len(ys) * n_row * PER_ROW * part * block * block,
            bytes_accessed=2 * len(ys) * n_row * PER_ROW * block * block,
            transcendentals=0,
        ),
        name="ahead_sums",
    )(*ys, *([packed] * len(ys)))


def step_kernel(has_got, has_acc, *refs):
    refs = list(refs)
    got_ref = refs.pop(0) if has_got else None
    acc_ref = refs.pop(0) if has_acc else None
    base_ref, inverse_ref, g_ref, y_ref, low_ref, out_ref = refs
    resid = base_ref[...]
    if has_got:
        resid = resid - jnp.sum(got_ref[...].astype(F32), axis=0)
    y = lax.dot_general(
        resid,
        inverse_ref[...],
        (((1,), (1,)), ((), ())),
        precision=HIGHEST,
        preferred_element_type=F32,
    )
    y_ref[...] = y
    low = y.astype(BF16)
    low_ref[...] = low
    n_row, block = g_ref.shape[0], g_ref.shape[-1]
    for r in range(n_row):
        new = times_row(low, g_ref[r])
        for a in range(PER_ROW):
            piece = new[:, a * block : (a + 1) * block]
            if has_acc:
                piece = piece + acc_ref[r, a]
            out_ref[a * n_row + r] = piece.astype(BF16)


def forward_step(got, acc, base, inverse, packed, first):
    n_row = packed.shape[0]
    part, block = base.shape
    whole_in = [x for x in (got, acc) if x is not None] + [base, inverse]
    return pl.pallas_call(
        functools.partial(step_kernel, got is not None, acc is not None),
        grid=(1,),
        in_specs=[whole(x.shape) for x in whole_in] + [column_spec(n_row, first, block)],
        out_specs=[
            whole((part, block)),
            whole((part, block)),
            whole((n_row * PER_ROW, part, block)),
        ],
        out_shape=[
            jax.ShapeDtypeStruct((part, block), F32),
            jax.ShapeDtypeStruct((part, block), BF16),
            jax.ShapeDtypeStruct((n_row * PER_ROW, part, block), BF16),
        ],
        cost_estimate=pl.CostEstimate(
            flops=2 * n_row * PER_ROW * part * block * block,
            bytes_accessed=2 * n_row * PER_ROW * block * block,
            transcendentals=0,
        ),
        name="forward_step",
    )(*whole_in, packed)


def near_kernel(x_ref, g_ref, rest_ref, inverse_ref, out_ref, low_ref):
    got = times_column(x_ref, g_ref, range(x_ref.shape[1]))
    solved = jnp.dot(
        rest_ref[...] - got, inverse_ref[...], precision=HIGHEST, preferred_element_type=F32
    )
    out_ref[...] = solved
    low_ref[...] = jnp.broadcast_to(solved.astype(BF16)[None], low_ref.shape)


def whole(shape):
    return pl.BlockSpec(shape, lambda s: (0,) * len(shape))


def column_spec(rows, first, block):
    return pl.BlockSpec((rows, PER_ROW, block, block), lambda s: (s, first, 0, 0))


def far_rest(y, xs, packed, firsts):
    n_row, part, block = xs[0].shape[1:]
    step = n_row // FAR_STEPS
    return pl.pallas_call(
        functools.partial(far_kernel, len(xs)),
        grid=(FAR_STEPS,),
        in_specs=[whole(y.shape)]
        + [whole(x.shape) for x in xs]
        + [column_spec(step, f, block) for f in firsts],
        out_specs=whole((part, block)),
        out_shape=jax.ShapeDtypeStruct((part, block), F32),
        cost_estimate=pl.CostEstimate(
            flops=2 * len(xs) * n_row * PER_ROW * part * block * block,
            bytes_accessed=2 * len(xs) * n_row * PER_ROW * block * block,
            transcendentals=0,
        ),
        name="far_rest",
    )(y, *xs, *([packed] * len(xs)))


def near_solve(x, packed, first, rest, inverse, n_col):
    n_row, part, block = x.shape[1:]
    return pl.pallas_call(
        near_kernel,
        grid=(1,),
        in_specs=[
            whole(x.shape),
            column_spec(n_row, first, block),
            whole(rest.shape),
            whole(inverse.shape),
        ],
        out_specs=[whole((part, block)), whole((n_col, part, block))],
        out_shape=[
            jax.ShapeDtypeStruct((part, block), F32),
            jax.ShapeDtypeStruct((n_col, part, block), BF16),
        ],
        cost_estimate=pl.CostEstimate(
            flops=2 * n_row * PER_ROW * part * block * block,
            bytes_accessed=2 * n_row * PER_ROW * block * block,
            transcendentals=0,
        ),
        name="near_solve",
    )(x, packed, rest, inverse)


def per_device(factor, pattern, loads, block_inverse):
    my_row = lax.axis_index("row")
    n_row = lax.axis_size("row")
    n_grp = lax.axis_size("grp")
    n_sub = lax.axis_size("sub")
    n_col = n_grp * n_sub
    scen = loads.shape[3]
    block = loads.shape[2]
    part = scen // n_row
    inverse = block_inverse[:, 0]
    loads_t = jnp.swapaxes(loads[:, 0], 1, 2)

    def forward_solve(level, resid):
        return lax.dot_general(
            resid, inverse[level], (((1,), (1,)), ((), ())), precision=HIGHEST
        )

    def backward_solve(level, resid):
        return lax.dot_general(
            resid, inverse[level], (((1,), (0,)), ((), ())), precision=HIGHEST
        )

    solved = [forward_solve(0, loads_t[0])]
    low = [solved[0].astype(BF16)]

    flags = pattern[:, 0, :, 0].astype(BF16)
    flags_after, low[0] = lax.optimization_barrier((flags, low[0]))

    def column(j, first, end, flags):
        rows = slice(first * PER_ROW, end * PER_ROW)
        return factor[rows, 0, j, 0] * flags[rows, j][:, None, None]

    columns = [column(j, j + 1, LEVELS, flags) for j in range(LEVELS - 1)]

    def crossing():
        blocks = [column(j, CROSS_FROM, LEVELS, flags_after) for j in range(CROSS_TO)]
        return lax.all_gather(jnp.stack(blocks), "sub", axis=0)

    place = {}
    for at_chunk, chunk in enumerate(CHUNKS):
        use = flags_after if at_chunk else flags
        packed = jnp.concatenate([column(j, a, b, use) for j, a, b in chunk], axis=0)
        packed = lax.all_gather(packed, "row", axis=0)
        at = 0
        for j, a, b in chunk:
            for t in range(a, b):
                place[t, j] = packed, at
                at += 1
        if at_chunk == 0:
            crossed = crossing()

    def local(t, m):
        return columns[m][(t - m - 1) * PER_ROW : (t - m) * PER_ROW]

    def local_sums(t, count):
        return sum(
            jnp.einsum("sq,apq->asp", low[m], local(t, m), preferred_element_type=F32)
            for m in range(count)
        ).astype(BF16)

    for t in range(1, NATIVE + 1):
        pieces = local_sums(t, t).reshape(n_col, part, block)
        total = jnp.sum(exchange(pieces, COL).astype(F32), axis=0).astype(BF16)
        total = exchange(spread(total, "row", n_row), "sub")
        total = total.reshape(scen, block).astype(F32)
        solved.append(forward_solve(t, loads_t[t] - total))
        low.append(solved[t].astype(BF16))

    pieces = jnp.stack(
        [local_sums(t, NATIVE + 1).reshape(n_col, part, block) for t in range(NATIVE + 1, LEVELS)],
        axis=1,
    )
    total = jnp.sum(exchange(pieces, COL).astype(F32), axis=0).astype(BF16)
    turn = [
        ((r * n_grp + g) * n_sub + k, (k * n_grp + g) * n_sub + r)
        for r in range(n_row)
        for g in range(n_grp)
        for k in range(n_sub)
    ]
    early = lax.ppermute(total, ALL, turn).astype(F32)

    def own(value):
        return lax.dynamic_slice_in_dim(value, my_row * part, part, axis=0)

    solved = [own(v) for v in solved]
    low = low + [None] * (LEVELS - NATIVE - 1)
    got = None
    for t in range(NATIVE + 1, LEVELS):
        base = own(loads_t[t]) - early[t - NATIVE - 1]
        if t < LEVELS - 1:
            acc = None
            before = range(NATIVE + 1, t)
            if before:
                acc = ahead_sums(
                    [low[m] for m in before],
                    place[t + 1, t][0],
                    [place[t + 1, m][1] for m in before],
                    n_row,
                )
            packed, at = place[t + 1, t]
            y, low[t], pieces = forward_step(got, acc, base, inverse[t], packed, at)
            got = exchange(pieces, COL)
        else:
            y = forward_solve(t, base - jnp.sum(got.astype(F32), axis=0))
        solved.append(y)

    out = [None] * LEVELS
    out[LEVELS - 1] = backward_solve(LEVELS - 1, solved[LEVELS - 1])
    wide = jnp.broadcast_to(out[LEVELS - 1].astype(BF16)[None], (n_col, part, block))
    later = []
    for j in reversed(range(LEVELS - 1)):
        rest = solved[j]
        if j < CROSS_TO:
            rest = rest - cross[j]
        far = [(t, x) for t, x in later if (t, j) in place]
        if far:
            rest = far_rest(
                rest, [x for _, x in far], place[far[0][0], j][0], [place[t, j][1] for t, _ in far]
            )
        near = exchange(wide, COL).reshape(PER_ROW, n_row, part, block)
        if j + 2 == CROSS_FROM:
            crossing_pieces, near = lax.optimization_barrier((crossing_pieces, near))
            cross = exchange(crossing_pieces, "row")
            cross = lax.ppermute(jnp.sum(cross.astype(F32), axis=0), ALL, turn)
        packed, at = place[j + 1, j]
        out[j], wide = near_solve(near, packed, at, rest, inverse[j], n_col)
        later.append((j + 1, near))
        if j + 1 == CROSS_FROM:
            mine = [
                lax.dynamic_index_in_dim(x, lax.axis_index("sub"), axis=1, keepdims=False)
                for _, x in reversed(later)
            ]
            mine, wide = lax.optimization_barrier((jnp.concatenate(mine, axis=0), wide))
            mine = lax.ppermute(mine, ALL, turn)
            crossing_pieces = cross_sums(mine, crossed)

    both = spread(jnp.stack(out).astype(BF16), "row", n_row)
    return jnp.transpose(both, (1, 3, 0, 2)).reshape(LEVELS, 1, block, scen).astype(F32)


def solution(mesh):
    n_col = mesh.shape["col"]
    n_row = mesh.shape["row"]
    devices = mesh.devices.reshape(n_row, n_col // SUB, SUB)
    in_specs = (
        P(None, "row", None, COL, None, None),
        P(None, "row", None, COL),
        P(None, COL, None, None),
        P(None, COL, None, None),
    )
    return jax.shard_map(
        per_device,
        mesh=Mesh(devices, ALL),
        in_specs=in_specs,
        out_specs=P(None, COL, None, None),
        check_vma=False,
    )
```

```python
import functools

import jax
import jax.numpy as jnp
from jax import lax
from jax.experimental import pallas as pl
from jax.experimental.pallas import tpu as pltpu
from jax.sharding import Mesh
from jax.sharding import PartitionSpec as P

LEVELS = 8
NATIVE = 2
FAR_STEPS = 2
PER_ROW = 4
SUB = 8
BF16 = jnp.bfloat16
F32 = jnp.float32
HIGHEST = lax.Precision.HIGHEST
COL = ("grp", "sub")
ALL = ("row", "grp", "sub")
CHUNKS = (
    ((6, 7, 8), (5, 6, 8), (4, 5, 8), (3, 4, 8)),
    ((2, 3, 8), (1, 2, 8), (0, 6, 8)),
    ((0, 1, 6),),
)


def exchange(pieces, axis):
    return lax.all_to_all(pieces, axis, 0, 0, tiled=True)


def spread(piece, axis, count):
    return exchange(jnp.broadcast_to(piece[None], (count,) + piece.shape), axis)


def times_column(x_ref, g_ref, rows):
    x = jnp.concatenate([x_ref[a, r] for r in rows for a in range(PER_ROW)], axis=1)
    g = g_ref[...].reshape(-1, g_ref.shape[-1])
    return jnp.dot(x, g, preferred_element_type=F32)


def far_kernel(count, *refs):
    y_ref, x_refs, g_refs, out_ref = refs[0], refs[1 : count + 1], refs[count + 1 : -1], refs[-1]
    n_row = x_refs[0].shape[1]
    step = n_row // FAR_STEPS
    for s in range(FAR_STEPS):

        @pl.when(pl.program_id(0) == s)
        def _():
            rows = range(s * step, (s + 1) * step)
            got = sum(times_column(x, g, rows) for x, g in zip(x_refs, g_refs))
            out_ref[...] = (y_ref[...] if s == 0 else out_ref[...]) - got


def near_kernel(count, steps, *refs):
    x_refs, g_refs = refs[:count], refs[count : 2 * count]
    rest_ref, inverse_ref, out_ref, low_ref, acc_ref = refs[2 * count :]
    step = x_refs[0].shape[1] // steps
    for s in range(steps):

        @pl.when(pl.program_id(0) == s)
        def _():
            rows = range(s * step, (s + 1) * step)
            got = sum(times_column(x, g, rows) for x, g in zip(x_refs, g_refs))
            rest = (rest_ref[...] if s == 0 else acc_ref[...]) - got
            if s < steps - 1:
                acc_ref[...] = rest
            else:
                solved = jnp.dot(
                    rest, inverse_ref[...], precision=HIGHEST, preferred_element_type=F32
                )
                out_ref[...] = solved
                low_ref[...] = jnp.broadcast_to(solved.astype(BF16)[None], low_ref.shape)


def pack_kernel(chunk, flags_ref, factor_ref, out_ref, sems):
    copies, at = [], 0
    for n, (j, a, b) in enumerate(chunk):
        size = (b - a) * PER_ROW
        copies.append(
            pltpu.make_async_copy(
                factor_ref.at[pl.ds(a * PER_ROW, size), j], out_ref.at[pl.ds(at, size)], sems.at[n]
            )
        )
        copies[-1].start()
        at += size
    at = 0
    for copy, (j, a, b) in zip(copies, chunk):
        copy.wait()
        for i in range((b - a) * PER_ROW):
            block = out_ref[at]
            out_ref[at] = jnp.where(flags_ref[a * PER_ROW + i, j] != 0, block, 0).astype(BF16)
            at += 1


def pack(chunk, factor, flags):
    count = sum(b - a for _, a, b in chunk) * PER_ROW
    shape = (count,) + factor.shape[2:]
    return pl.pallas_call(
        functools.partial(pack_kernel, chunk),
        in_specs=[
            pl.BlockSpec(memory_space=pltpu.SMEM),
            pl.BlockSpec(memory_space=pl.ANY),
        ],
        out_specs=pl.BlockSpec(memory_space=pltpu.VMEM),
        out_shape=jax.ShapeDtypeStruct(shape, factor.dtype),
        scratch_shapes=[pltpu.SemaphoreType.DMA((len(chunk),))],
        cost_estimate=pl.CostEstimate(
            flops=count * shape[1] * shape[2],
            bytes_accessed=4 * count * shape[1] * shape[2],
            transcendentals=0,
        ),
        name="pack",
    )(flags, factor)


def whole(shape):
    return pl.BlockSpec(shape, lambda s: (0,) * len(shape))


def column_spec(rows, first, block):
    return pl.BlockSpec((rows, PER_ROW, block, block), lambda s: (s, first, 0, 0))


def far_rest(y, xs, packed, firsts):
    n_row, part, block = xs[0].shape[1:]
    step = n_row // FAR_STEPS
    return pl.pallas_call(
        functools.partial(far_kernel, len(xs)),
        grid=(FAR_STEPS,),
        in_specs=[whole(y.shape)]
        + [whole(x.shape) for x in xs]
        + [column_spec(step, f, block) for f in firsts],
        out_specs=whole((part, block)),
        out_shape=jax.ShapeDtypeStruct((part, block), F32),
        cost_estimate=pl.CostEstimate(
            flops=2 * len(xs) * n_row * PER_ROW * part * block * block,
            bytes_accessed=2 * len(xs) * n_row * PER_ROW * block * block,
            transcendentals=0,
        ),
        name="far_rest",
    )(y, *xs, *([packed] * len(xs)))


def near_solve(xs, packed, firsts, rest, inverse, n_col):
    n_row, part, block = xs[0].shape[1:]
    steps = 1 if len(xs) == 1 else FAR_STEPS
    return pl.pallas_call(
        functools.partial(near_kernel, len(xs), steps),
        grid=(steps,),
        in_specs=[whole(x.shape) for x in xs]
        + [column_spec(n_row // steps, f, block) for f in firsts]
        + [whole(rest.shape), whole(inverse.shape)],
        out_specs=[whole((part, block)), whole((n_col, part, block))],
        out_shape=[
            jax.ShapeDtypeStruct((part, block), F32),
            jax.ShapeDtypeStruct((n_col, part, block), BF16),
        ],
        scratch_shapes=[pltpu.VMEM((part, block), F32)],
        cost_estimate=pl.CostEstimate(
            flops=2 * len(xs) * n_row * PER_ROW * part * block * block,
            bytes_accessed=2 * len(xs) * n_row * PER_ROW * block * block,
            transcendentals=0,
        ),
        name="near_solve",
    )(*xs, *([packed] * len(xs)), rest, inverse)


def per_device(factor, pattern, loads, block_inverse):
    my_row = lax.axis_index("row")
    n_row = lax.axis_size("row")
    n_grp = lax.axis_size("grp")
    n_sub = lax.axis_size("sub")
    n_col = n_grp * n_sub
    scen = loads.shape[3]
    block = loads.shape[2]
    part = scen // n_row
    inverse = block_inverse[:, 0]
    loads_t = jnp.swapaxes(loads[:, 0], 1, 2)

    def forward_solve(level, resid):
        return lax.dot_general(
            resid, inverse[level], (((1,), (1,)), ((), ())), precision=HIGHEST
        )

    def backward_solve(level, resid):
        return lax.dot_general(
            resid, inverse[level], (((1,), (0,)), ((), ())), precision=HIGHEST
        )

    solved = [forward_solve(0, loads_t[0])]
    low = [solved[0].astype(BF16)]

    columns = []
    for j in range(NATIVE + 1):
        rows = slice((j + 1) * PER_ROW, LEVELS * PER_ROW)
        columns.append(factor[rows, 0, j, 0] * pattern[rows, 0, j, 0].astype(BF16)[:, None, None])

    flags = pattern[:, 0, :, 0]
    flags_after, low[0] = lax.optimization_barrier((flags, low[0]))
    place = {}
    for number, chunk in enumerate(CHUNKS):
        packed = pack(chunk, factor[:, 0, :, 0], flags_after if number else flags)
        packed = lax.all_gather(packed, "row", axis=0)
        at = 0
        for j, a, b in chunk:
            for t in range(a, b):
                place[t, j] = packed, at
                at += 1

    def local(t, m):
        return columns[m][(t - m - 1) * PER_ROW : (t - m) * PER_ROW]

    def split(t, m):
        packed, at = place[t, m]
        return packed[:, at * PER_ROW : (at + 1) * PER_ROW]

    def local_sums(t, count):
        return sum(
            jnp.einsum("sq,apq->asp", low[m], local(t, m), preferred_element_type=F32)
            for m in range(count)
        ).astype(BF16)

    for t in range(1, NATIVE + 1):
        pieces = local_sums(t, t).reshape(n_col, part, block)
        total = jnp.sum(exchange(pieces, COL).astype(F32), axis=0).astype(BF16)
        total = exchange(spread(total, "row", n_row), "sub")
        total = total.reshape(scen, block).astype(F32)
        solved.append(forward_solve(t, loads_t[t] - total))
        low.append(solved[t].astype(BF16))

    pieces = jnp.stack(
        [local_sums(t, NATIVE + 1).reshape(n_col, part, block) for t in range(NATIVE + 1, LEVELS)],
        axis=1,
    )
    total = jnp.sum(exchange(pieces, COL).astype(F32), axis=0).astype(BF16)
    turn = [
        ((r * n_grp + g) * n_sub + k, (k * n_grp + g) * n_sub + r)
        for r in range(n_row)
        for g in range(n_grp)
        for k in range(n_sub)
    ]
    early = lax.ppermute(total, ALL, turn).astype(F32)

    def own(value):
        return lax.dynamic_slice_in_dim(value, my_row * part, part, axis=0)

    solved = [own(v) for v in solved]
    low = low + [None] * (LEVELS - NATIVE - 1)
    for t in range(NATIVE + 1, LEVELS):
        total = early[t - NATIVE - 1]
        if t > NATIVE + 1:
            sums = sum(
                jnp.einsum("sq,rapq->arsp", low[m], split(t, m), preferred_element_type=F32)
                for m in range(NATIVE + 1, t)
            )
            pieces = sums.astype(BF16).reshape(n_col, part, block)
            total = total + jnp.sum(exchange(pieces, COL).astype(F32), axis=0)
        solved.append(forward_solve(t, own(loads_t[t]) - total))
        low[t] = solved[t].astype(BF16)

    out = [None] * LEVELS
    out[LEVELS - 1] = backward_solve(LEVELS - 1, solved[LEVELS - 1])
    wide = jnp.broadcast_to(out[LEVELS - 1].astype(BF16)[None], (n_col, part, block))
    later = []
    for j in reversed(range(LEVELS - 1)):
        rest, packed = solved[j], place[j + 1, j][0]
        joined = [(t, x) for t, x in later if j == 0 and place[t, j][0] is packed]
        far = later[: len(later) - len(joined)]
        if far:
            rest = far_rest(
                rest,
                [x for _, x in far],
                place[far[0][0], j][0],
                [place[t, j][1] for t, _ in far],
            )
        near = exchange(wide, COL).reshape(PER_ROW, n_row, part, block)
        joined.append((j + 1, near))
        out[j], wide = near_solve(
            [x for _, x in joined],
            packed,
            [place[t, j][1] for t, _ in joined],
            rest,
            inverse[j],
            n_col,
        )
        later.append((j + 1, near))

    both = spread(jnp.stack(out).astype(BF16), "row", n_row)
    return jnp.transpose(both, (1, 3, 0, 2)).reshape(LEVELS, 1, block, scen).astype(F32)


def solution(mesh):
    n_col = mesh.shape["col"]
    n_row = mesh.shape["row"]
    devices = mesh.devices.reshape(n_row, n_col // SUB, SUB)
    in_specs = (
        P(None, "row", None, COL, None, None),
        P(None, "row", None, COL),
        P(None, COL, None, None),
        P(None, COL, None, None),
    )
    return jax.shard_map(
        per_device,
        mesh=Mesh(devices, ALL),
        in_specs=in_specs,
        out_specs=P(None, COL, None, None),
        check_vma=False,
    )
```

```python
import functools

import jax
import jax.numpy as jnp
from jax import lax
from jax.experimental import pallas as pl
from jax.experimental.pallas import tpu as pltpu
from jax.sharding import Mesh
from jax.sharding import PartitionSpec as P

LEVELS = 8
NATIVE = 2
FAR_STEPS = 2
OUT_SPLIT = 3
PER_ROW = 4
SUB = 8
BF16 = jnp.bfloat16
F32 = jnp.float32
HIGHEST = lax.Precision.HIGHEST
COL = ("grp", "sub")
ALL = ("row", "grp", "sub")
CHUNKS = (
    ((6, 7, 8), (5, 6, 8), (4, 5, 8), (3, 4, 8)),
    ((2, 3, 8), (1, 2, 8), (0, 6, 8)),
    ((0, 1, 6),),
)


def exchange(pieces, axis):
    return lax.all_to_all(pieces, axis, 0, 0, tiled=True)


def spread(piece, axis, count):
    return exchange(jnp.broadcast_to(piece[None], (count,) + piece.shape), axis)


def times_column(x_ref, g_ref, rows):
    x = jnp.concatenate([x_ref[a, r] for r in rows for a in range(PER_ROW)], axis=1)
    g = g_ref[...].reshape(-1, g_ref.shape[-1])
    return jnp.dot(x, g, preferred_element_type=F32)


def far_kernel(count, *refs):
    y_ref, x_refs, g_refs, out_ref = refs[0], refs[1 : count + 1], refs[count + 1 : -1], refs[-1]
    n_row = x_refs[0].shape[1]
    step = n_row // FAR_STEPS
    for s in range(FAR_STEPS):

        @pl.when(pl.program_id(0) == s)
        def _():
            rows = range(s * step, (s + 1) * step)
            got = sum(times_column(x, g, rows) for x, g in zip(x_refs, g_refs))
            out_ref[...] = (y_ref[...] if s == 0 else out_ref[...]) - got


def near_kernel(count, steps, *refs):
    x_refs, g_refs = refs[:count], refs[count : 2 * count]
    rest_ref, inverse_ref, out_ref, low_ref, acc_ref = refs[2 * count :]
    step = x_refs[0].shape[1] // steps
    for s in range(steps):

        @pl.when(pl.program_id(0) == s)
        def _():
            rows = range(s * step, (s + 1) * step)
            got = sum(times_column(x, g, rows) for x, g in zip(x_refs, g_refs))
            rest = (rest_ref[...] if s == 0 else acc_ref[...]) - got
            if s < steps - 1:
                acc_ref[...] = rest
            else:
                solved = jnp.dot(
                    rest, inverse_ref[...], precision=HIGHEST, preferred_element_type=F32
                )
                out_ref[...] = solved
                low_ref[...] = jnp.broadcast_to(solved.astype(BF16)[None], low_ref.shape)


def pack_kernel(chunk, flags_ref, factor_ref, out_ref, sems):
    copies, at = [], 0
    for n, (j, a, b) in enumerate(chunk):
        size = (b - a) * PER_ROW
        copies.append(
            pltpu.make_async_copy(
                factor_ref.at[pl.ds(a * PER_ROW, size), j], out_ref.at[pl.ds(at, size)], sems.at[n]
            )
        )
        copies[-1].start()
        at += size
    at = 0
    for copy, (j, a, b) in zip(copies, chunk):
        copy.wait()
        for i in range((b - a) * PER_ROW):
            block = out_ref[at]
            out_ref[at] = jnp.where(flags_ref[a * PER_ROW + i, j] != 0, block, 0).astype(BF16)
            at += 1


def pack(chunk, factor, flags):
    count = sum(b - a for _, a, b in chunk) * PER_ROW
    shape = (count,) + factor.shape[2:]
    return pl.pallas_call(
        functools.partial(pack_kernel, chunk),
        in_specs=[
            pl.BlockSpec(memory_space=pltpu.SMEM),
            pl.BlockSpec(memory_space=pl.ANY),
        ],
        out_specs=pl.BlockSpec(memory_space=pltpu.VMEM),
        out_shape=jax.ShapeDtypeStruct(shape, factor.dtype),
        scratch_shapes=[pltpu.SemaphoreType.DMA((len(chunk),))],
        cost_estimate=pl.CostEstimate(
            flops=count * shape[1] * shape[2],
            bytes_accessed=4 * count * shape[1] * shape[2],
            transcendentals=0,
        ),
        name="pack",
    )(flags, factor)


def whole(shape):
    return pl.BlockSpec(shape, lambda s: (0,) * len(shape))


def column_spec(rows, first, block):
    return pl.BlockSpec((rows, PER_ROW, block, block), lambda s: (s, first, 0, 0))


def far_rest(y, xs, packed, firsts):
    n_row, part, block = xs[0].shape[1:]
    step = n_row // FAR_STEPS
    return pl.pallas_call(
        functools.partial(far_kernel, len(xs)),
        grid=(FAR_STEPS,),
        in_specs=[whole(y.shape)]
        + [whole(x.shape) for x in xs]
        + [column_spec(step, f, block) for f in firsts],
        out_specs=whole((part, block)),
        out_shape=jax.ShapeDtypeStruct((part, block), F32),
        cost_estimate=pl.CostEstimate(
            flops=2 * len(xs) * n_row * PER_ROW * part * block * block,
            bytes_accessed=2 * len(xs) * n_row * PER_ROW * block * block,
            transcendentals=0,
        ),
        name="far_rest",
    )(y, *xs, *([packed] * len(xs)))


def near_solve(xs, packed, firsts, rest, inverse, n_col):
    n_row, part, block = xs[0].shape[1:]
    steps = 1 if len(xs) == 1 else FAR_STEPS
    return pl.pallas_call(
        functools.partial(near_kernel, len(xs), steps),
        grid=(steps,),
        in_specs=[whole(x.shape) for x in xs]
        + [column_spec(n_row // steps, f, block) for f in firsts]
        + [whole(rest.shape), whole(inverse.shape)],
        out_specs=[whole((part, block)), whole((n_col, part, block))],
        out_shape=[
            jax.ShapeDtypeStruct((part, block), F32),
            jax.ShapeDtypeStruct((n_col, part, block), BF16),
        ],
        scratch_shapes=[pltpu.VMEM((part, block), F32)],
        cost_estimate=pl.CostEstimate(
            flops=2 * len(xs) * n_row * PER_ROW * part * block * block,
            bytes_accessed=2 * len(xs) * n_row * PER_ROW * block * block,
            transcendentals=0,
        ),
        name="near_solve",
    )(*xs, *([packed] * len(xs)), rest, inverse)


def per_device(factor, pattern, loads, block_inverse):
    my_row = lax.axis_index("row")
    n_row = lax.axis_size("row")
    n_grp = lax.axis_size("grp")
    n_sub = lax.axis_size("sub")
    n_col = n_grp * n_sub
    scen = loads.shape[3]
    block = loads.shape[2]
    part = scen // n_row
    inverse = block_inverse[:, 0]
    loads_t = jnp.swapaxes(loads[:, 0], 1, 2)

    def forward_solve(level, resid):
        return lax.dot_general(
            resid, inverse[level], (((1,), (1,)), ((), ())), precision=HIGHEST
        )

    def backward_solve(level, resid):
        return lax.dot_general(
            resid, inverse[level], (((1,), (0,)), ((), ())), precision=HIGHEST
        )

    solved = [forward_solve(0, loads_t[0])]
    low = [solved[0].astype(BF16)]

    columns = []
    for j in range(NATIVE + 1):
        rows = slice((j + 1) * PER_ROW, LEVELS * PER_ROW)
        columns.append(factor[rows, 0, j, 0] * pattern[rows, 0, j, 0].astype(BF16)[:, None, None])

    flags = pattern[:, 0, :, 0]
    flags_after, low[0] = lax.optimization_barrier((flags, low[0]))
    place = {}
    for number, chunk in enumerate(CHUNKS):
        packed = pack(chunk, factor[:, 0, :, 0], flags_after if number else flags)
        packed = lax.all_gather(packed, "row", axis=0)
        at = 0
        for j, a, b in chunk:
            for t in range(a, b):
                place[t, j] = packed, at
                at += 1

    def local(t, m):
        return columns[m][(t - m - 1) * PER_ROW : (t - m) * PER_ROW]

    def split(t, m):
        packed, at = place[t, m]
        return packed[:, at * PER_ROW : (at + 1) * PER_ROW]

    def local_sums(t, count):
        return sum(
            jnp.einsum("sq,apq->asp", low[m], local(t, m), preferred_element_type=F32)
            for m in range(count)
        ).astype(BF16)

    for t in range(1, NATIVE + 1):
        pieces = local_sums(t, t).reshape(n_col, part, block)
        total = jnp.sum(exchange(pieces, COL).astype(F32), axis=0).astype(BF16)
        total = exchange(spread(total, "row", n_row), "sub")
        total = total.reshape(scen, block).astype(F32)
        solved.append(forward_solve(t, loads_t[t] - total))
        low.append(solved[t].astype(BF16))

    pieces = jnp.stack(
        [local_sums(t, NATIVE + 1).reshape(n_col, part, block) for t in range(NATIVE + 1, LEVELS)],
        axis=1,
    )
    total = jnp.sum(exchange(pieces, COL).astype(F32), axis=0).astype(BF16)
    turn = [
        ((r * n_grp + g) * n_sub + k, (k * n_grp + g) * n_sub + r)
        for r in range(n_row)
        for g in range(n_grp)
        for k in range(n_sub)
    ]
    early = lax.ppermute(total, ALL, turn).astype(F32)

    def own(value):
        return lax.dynamic_slice_in_dim(value, my_row * part, part, axis=0)

    solved = [own(v) for v in solved]
    low = low + [None] * (LEVELS - NATIVE - 1)
    for t in range(NATIVE + 1, LEVELS):
        total = early[t - NATIVE - 1]
        if t > NATIVE + 1:
            sums = sum(
                jnp.einsum("sq,rapq->arsp", low[m], split(t, m), preferred_element_type=F32)
                for m in range(NATIVE + 1, t)
            )
            pieces = sums.astype(BF16).reshape(n_col, part, block)
            total = total + jnp.sum(exchange(pieces, COL).astype(F32), axis=0)
        solved.append(forward_solve(t, own(loads_t[t]) - total))
        low[t] = solved[t].astype(BF16)

    out = [None] * LEVELS
    out[LEVELS - 1] = backward_solve(LEVELS - 1, solved[LEVELS - 1])
    wide = jnp.broadcast_to(out[LEVELS - 1].astype(BF16)[None], (n_col, part, block))
    later = []
    for j in reversed(range(LEVELS - 1)):
        rest, packed = solved[j], place[j + 1, j][0]
        joined = [(t, x) for t, x in later if j == 0 and place[t, j][0] is packed]
        far = later[: len(later) - len(joined)]
        if far:
            rest = far_rest(
                rest,
                [x for _, x in far],
                place[far[0][0], j][0],
                [place[t, j][1] for t, _ in far],
            )
        near = exchange(wide, COL).reshape(PER_ROW, n_row, part, block)
        joined.append((j + 1, near))
        out[j], wide = near_solve(
            [x for _, x in joined],
            packed,
            [place[t, j][1] for t, _ in joined],
            rest,
            inverse[j],
            n_col,
        )
        later.append((j + 1, near))
        if j == OUT_SPLIT:
            upper = spread(jnp.stack(out[j:]).astype(BF16), "row", n_row)
            upper, wide = lax.optimization_barrier((upper, wide))

    lower = spread(jnp.stack(out[:OUT_SPLIT]).astype(BF16), "row", n_row)
    both = jnp.concatenate([lower, upper], axis=1)
    return jnp.transpose(both, (1, 3, 0, 2)).reshape(LEVELS, 1, block, scen).astype(F32)


def solution(mesh):
    n_col = mesh.shape["col"]
    n_row = mesh.shape["row"]
    devices = mesh.devices.reshape(n_row, n_col // SUB, SUB)
    in_specs = (
        P(None, "row", None, COL, None, None),
        P(None, "row", None, COL),
        P(None, COL, None, None),
        P(None, COL, None, None),
    )
    return jax.shard_map(
        per_device,
        mesh=Mesh(devices, ALL),
        in_specs=in_specs,
        out_specs=P(None, COL, None, None),
        check_vma=False,
    )
```

```python
import functools

import jax
import jax.numpy as jnp
from jax import lax
from jax.experimental import pallas as pl
from jax.experimental.pallas import tpu as pltpu
from jax.sharding import Mesh
from jax.sharding import PartitionSpec as P

LEVELS = 8
NATIVE = 2
FAR_STEPS = 2
OUT_SPLIT = 3
PER_ROW = 4
SUB = 8
BF16 = jnp.bfloat16
F32 = jnp.float32
HIGHEST = lax.Precision.HIGHEST
COL = ("grp", "sub")
ALL = ("row", "grp", "sub")
CHUNKS = (
    ((6, 7, 8), (5, 6, 8), (4, 5, 8), (3, 4, 8)),
    ((2, 3, 8), (1, 2, 8), (0, 6, 8)),
    ((0, 1, 6),),
)


def exchange(pieces, axis):
    return lax.all_to_all(pieces, axis, 0, 0, tiled=True)


def spread(piece, axis, count):
    return exchange(jnp.broadcast_to(piece[None], (count,) + piece.shape), axis)


def times_column(x_ref, g_ref, rows):
    x = jnp.concatenate([x_ref[a, r] for r in rows for a in range(PER_ROW)], axis=1)
    g = g_ref[...].reshape(-1, g_ref.shape[-1])
    return jnp.dot(x, g, preferred_element_type=F32)


def far_kernel(count, *refs):
    y_ref, x_refs, g_refs, out_ref = refs[0], refs[1 : count + 1], refs[count + 1 : -1], refs[-1]
    n_row = x_refs[0].shape[1]
    step = n_row // FAR_STEPS
    for s in range(FAR_STEPS):

        @pl.when(pl.program_id(0) == s)
        def _():
            rows = range(s * step, (s + 1) * step)
            got = sum(times_column(x, g, rows) for x, g in zip(x_refs, g_refs))
            out_ref[...] = (y_ref[...] if s == 0 else out_ref[...]) - got


def near_kernel(count, steps, *refs):
    x_refs, g_refs = refs[:count], refs[count : 2 * count]
    rest_ref, inverse_ref, out_ref, low_ref, acc_ref = refs[2 * count :]
    step = x_refs[0].shape[1] // steps
    for s in range(steps):

        @pl.when(pl.program_id(0) == s)
        def _():
            rows = range(s * step, (s + 1) * step)
            got = sum(times_column(x, g, rows) for x, g in zip(x_refs, g_refs))
            rest = (rest_ref[...] if s == 0 else acc_ref[...]) - got
            if s < steps - 1:
                acc_ref[...] = rest
            else:
                solved = jnp.dot(
                    rest, inverse_ref[...], precision=HIGHEST, preferred_element_type=F32
                )
                out_ref[...] = solved
                low_ref[...] = jnp.broadcast_to(solved.astype(BF16)[None], low_ref.shape)


def pack_kernel(chunk, flags_ref, factor_ref, out_ref, sems):
    copies, at = [], 0
    for n, (j, a, b) in enumerate(chunk):
        size = (b - a) * PER_ROW
        copies.append(
            pltpu.make_async_copy(
                factor_ref.at[pl.ds(a * PER_ROW, size), j], out_ref.at[pl.ds(at, size)], sems.at[n]
            )
        )
        copies[-1].start()
        at += size
    at = 0
    for copy, (j, a, b) in zip(copies, chunk):
        copy.wait()
        for i in range((b - a) * PER_ROW):
            block = out_ref[at]
            out_ref[at] = jnp.where(flags_ref[j, a * PER_ROW + i] != 0, block, 0).astype(BF16)
            at += 1


def pack(chunk, factor, flags):
    count = sum(b - a for _, a, b in chunk) * PER_ROW
    shape = (count,) + factor.shape[2:]
    return pl.pallas_call(
        functools.partial(pack_kernel, chunk),
        in_specs=[
            pl.BlockSpec(memory_space=pltpu.SMEM),
            pl.BlockSpec(memory_space=pl.ANY),
        ],
        out_specs=pl.BlockSpec(memory_space=pltpu.VMEM),
        out_shape=jax.ShapeDtypeStruct(shape, factor.dtype),
        scratch_shapes=[pltpu.SemaphoreType.DMA((len(chunk),))],
        cost_estimate=pl.CostEstimate(
            flops=count * shape[1] * shape[2],
            bytes_accessed=4 * count * shape[1] * shape[2],
            transcendentals=0,
        ),
        name="pack",
    )(flags, factor)


def near_memory(x):
    return pltpu.with_memory_space_constraint(x, pltpu.VMEM)


def whole(shape):
    return pl.BlockSpec(memory_space=pltpu.VMEM)


def column_spec(rows, first, block):
    return pl.BlockSpec((rows, PER_ROW, block, block), lambda s: (s, first, 0, 0))


def far_rest(y, xs, packed, firsts):
    n_row, part, block = xs[0].shape[1:]
    step = n_row // FAR_STEPS
    return pl.pallas_call(
        functools.partial(far_kernel, len(xs)),
        grid=(FAR_STEPS,),
        in_specs=[whole(y.shape)]
        + [whole(x.shape) for x in xs]
        + [column_spec(step, f, block) for f in firsts],
        out_specs=whole((part, block)),
        out_shape=pltpu.VMEM((part, block), F32),
        cost_estimate=pl.CostEstimate(
            flops=2 * len(xs) * n_row * PER_ROW * part * block * block,
            bytes_accessed=2 * len(xs) * n_row * PER_ROW * block * block,
            transcendentals=0,
        ),
        name="far_rest",
    )(near_memory(y), *map(near_memory, xs), *([packed] * len(xs)))


def near_solve(xs, packed, firsts, rest, inverse, n_col):
    n_row, part, block = xs[0].shape[1:]
    steps = 1 if len(xs) == 1 else FAR_STEPS
    return pl.pallas_call(
        functools.partial(near_kernel, len(xs), steps),
        grid=(steps,),
        in_specs=[whole(x.shape) for x in xs]
        + [column_spec(n_row // steps, f, block) for f in firsts]
        + [whole(rest.shape), whole(inverse.shape)],
        out_specs=[whole((part, block)), whole((n_col, part, block))],
        out_shape=[
            pltpu.VMEM((part, block), F32),
            pltpu.VMEM((n_col, part, block), BF16),
        ],
        scratch_shapes=[pltpu.VMEM((part, block), F32)],
        cost_estimate=pl.CostEstimate(
            flops=2 * len(xs) * n_row * PER_ROW * part * block * block,
            bytes_accessed=2 * len(xs) * n_row * PER_ROW * block * block,
            transcendentals=0,
        ),
        name="near_solve",
    )(*map(near_memory, xs), *([packed] * len(xs)), near_memory(rest), near_memory(inverse))


def per_device(factor, pattern, loads, block_inverse):
    my_row = lax.axis_index("row")
    n_row = lax.axis_size("row")
    n_grp = lax.axis_size("grp")
    n_sub = lax.axis_size("sub")
    n_col = n_grp * n_sub
    scen = loads.shape[3]
    block = loads.shape[2]
    part = scen // n_row
    inverse = block_inverse[:, 0]
    loads_t = jnp.swapaxes(loads[:, 0], 1, 2)

    def forward_solve(level, resid):
        return lax.dot_general(
            resid, inverse[level], (((1,), (1,)), ((), ())), precision=HIGHEST
        )

    def backward_solve(level, resid):
        return lax.dot_general(
            resid, inverse[level], (((1,), (0,)), ((), ())), precision=HIGHEST
        )

    solved = [forward_solve(0, loads_t[0])]
    low = [solved[0].astype(BF16)]

    columns = []
    for j in range(NATIVE + 1):
        rows = slice((j + 1) * PER_ROW, LEVELS * PER_ROW)
        columns.append(factor[rows, 0, j, 0] * pattern[rows, 0, j, 0].astype(BF16)[:, None, None])

    flags = pattern[:, 0, :, 0].T
    flags_after, low[0] = lax.optimization_barrier((flags, low[0]))
    place = {}
    for number, chunk in enumerate(CHUNKS):
        packed = pack(chunk, factor[:, 0, :, 0], flags_after if number else flags)
        packed = lax.all_gather(packed, "row", axis=0)
        at = 0
        for j, a, b in chunk:
            for t in range(a, b):
                place[t, j] = packed, at
                at += 1

    def local(t, m):
        return columns[m][(t - m - 1) * PER_ROW : (t - m) * PER_ROW]

    def split(t, m):
        packed, at = place[t, m]
        return packed[:, at * PER_ROW : (at + 1) * PER_ROW]

    def local_sums(t, count):
        return sum(
            jnp.einsum("sq,apq->asp", low[m], local(t, m), preferred_element_type=F32)
            for m in range(count)
        ).astype(BF16)

    for t in range(1, NATIVE + 1):
        pieces = local_sums(t, t).reshape(n_col, part, block)
        total = jnp.sum(exchange(pieces, COL).astype(F32), axis=0).astype(BF16)
        total = exchange(spread(total, "row", n_row), "sub")
        total = total.reshape(scen, block).astype(F32)
        solved.append(forward_solve(t, loads_t[t] - total))
        low.append(solved[t].astype(BF16))

    pieces = jnp.stack(
        [local_sums(t, NATIVE + 1).reshape(n_col, part, block) for t in range(NATIVE + 1, LEVELS)],
        axis=1,
    )
    total = jnp.sum(exchange(pieces, COL).astype(F32), axis=0).astype(BF16)
    turn = [
        ((r * n_grp + g) * n_sub + k, (k * n_grp + g) * n_sub + r)
        for r in range(n_row)
        for g in range(n_grp)
        for k in range(n_sub)
    ]
    early = lax.ppermute(total, ALL, turn).astype(F32)

    def own(value):
        return lax.dynamic_slice_in_dim(value, my_row * part, part, axis=0)

    solved = [own(v) for v in solved]
    low = low + [None] * (LEVELS - NATIVE - 1)
    for t in range(NATIVE + 1, LEVELS):
        total = early[t - NATIVE - 1]
        if t > NATIVE + 1:
            sums = sum(
                jnp.einsum("sq,rapq->arsp", low[m], split(t, m), preferred_element_type=F32)
                for m in range(NATIVE + 1, t)
            )
            pieces = sums.astype(BF16).reshape(n_col, part, block)
            total = total + jnp.sum(exchange(pieces, COL).astype(F32), axis=0)
        solved.append(forward_solve(t, own(loads_t[t]) - total))
        low[t] = solved[t].astype(BF16)

    out = [None] * LEVELS
    out[LEVELS - 1] = backward_solve(LEVELS - 1, solved[LEVELS - 1])
    wide = jnp.broadcast_to(out[LEVELS - 1].astype(BF16)[None], (n_col, part, block))
    later = []
    for j in reversed(range(LEVELS - 1)):
        rest, packed = solved[j], place[j + 1, j][0]
        joined = [(t, x) for t, x in later if j == 0 and place[t, j][0] is packed]
        far = later[: len(later) - len(joined)]
        if far:
            rest = far_rest(
                rest,
                [x for _, x in far],
                place[far[0][0], j][0],
                [place[t, j][1] for t, _ in far],
            )
        if j == OUT_SPLIT - 1:
            upper, rest = lax.optimization_barrier((jnp.stack(out[j + 1 :]).astype(BF16), rest))
            upper, wide = lax.optimization_barrier((spread(upper, "row", n_row), wide))
        near = exchange(wide, COL).reshape(PER_ROW, n_row, part, block)
        joined.append((j + 1, near))
        out[j], wide = near_solve(
            [x for _, x in joined],
            packed,
            [place[t, j][1] for t, _ in joined],
            rest,
            inverse[j],
            n_col,
        )
        later.append((j + 1, near))

    lower = spread(jnp.stack(out[:OUT_SPLIT]).astype(BF16), "row", n_row)
    both = jnp.concatenate([lower, upper], axis=1)
    return jnp.transpose(both, (1, 3, 0, 2)).reshape(LEVELS, 1, block, scen).astype(F32)


def solution(mesh):
    n_col = mesh.shape["col"]
    n_row = mesh.shape["row"]
    devices = mesh.devices.reshape(n_row, n_col // SUB, SUB)
    in_specs = (
        P(None, "row", None, COL, None, None),
        P(None, "row", None, COL),
        P(None, COL, None, None),
        P(None, COL, None, None),
    )
    return jax.shard_map(
        per_device,
        mesh=Mesh(devices, ALL),
        in_specs=in_specs,
        out_specs=P(None, COL, None, None),
        check_vma=False,
    )
```

```python
import functools

import jax
import jax.numpy as jnp
from jax import lax
from jax.experimental import pallas as pl
from jax.experimental.pallas import tpu as pltpu
from jax.sharding import Mesh
from jax.sharding import PartitionSpec as P

LEVELS = 8
NATIVE = 2
FAR_STEPS = 2
OUT_SPLIT = 3
PER_ROW = 4
SUB = 8
BF16 = jnp.bfloat16
F32 = jnp.float32
HIGHEST = lax.Precision.HIGHEST
COL = ("grp", "sub")
ALL = ("row", "grp", "sub")
CHUNKS = (
    ((6, 7, 8), (5, 6, 8), (4, 5, 8), (3, 4, 8)),
    ((2, 3, 8), (1, 2, 8), (0, 6, 8)),
    ((0, 1, 6),),
)


def exchange(pieces, axis):
    return lax.all_to_all(pieces, axis, 0, 0, tiled=True)


def spread(piece, axis, count):
    return exchange(jnp.broadcast_to(piece[None], (count,) + piece.shape), axis)


def times_column(x_ref, g_ref, rows):
    x = jnp.concatenate([x_ref[a, r] for r in rows for a in range(PER_ROW)], axis=1)
    g = g_ref[...].reshape(-1, g_ref.shape[-1])
    return jnp.dot(x, g, preferred_element_type=F32)


def far_kernel(count, *refs):
    y_ref, x_refs, g_refs, out_ref = refs[0], refs[1 : count + 1], refs[count + 1 : -1], refs[-1]
    n_row = x_refs[0].shape[1]
    step = n_row // FAR_STEPS
    for s in range(FAR_STEPS):

        @pl.when(pl.program_id(0) == s)
        def _():
            rows = range(s * step, (s + 1) * step)
            got = sum(times_column(x, g, rows) for x, g in zip(x_refs, g_refs))
            out_ref[...] = (y_ref[...] if s == 0 else out_ref[...]) - got


def near_kernel(count, steps, *refs):
    x_refs, g_refs = refs[:count], refs[count : 2 * count]
    rest_ref, inverse_ref, out_ref, low_ref, acc_ref = refs[2 * count :]
    step = x_refs[0].shape[1] // steps
    for s in range(steps):

        @pl.when(pl.program_id(0) == s)
        def _():
            rows = range(s * step, (s + 1) * step)
            got = sum(times_column(x, g, rows) for x, g in zip(x_refs, g_refs))
            rest = (rest_ref[...] if s == 0 else acc_ref[...]) - got
            if s < steps - 1:
                acc_ref[...] = rest
            else:
                solved = jnp.dot(
                    rest, inverse_ref[...], precision=HIGHEST, preferred_element_type=F32
                )
                out_ref[...] = solved
                low_ref[...] = jnp.broadcast_to(solved.astype(BF16)[None], low_ref.shape)


def pack_kernel(chunk, flags_ref, factor_ref, out_ref, held_ref, in_sems, out_sems):
    ins, outs, at = [], [], 0
    for n, (j, a, b) in enumerate(chunk):
        size = (b - a) * PER_ROW
        held = held_ref.at[pl.ds(at, size)]
        ins.append(
            pltpu.make_async_copy(
                factor_ref.at[pl.ds(a * PER_ROW, size), j], held, in_sems.at[n]
            )
        )
        outs.append(pltpu.make_async_copy(held, out_ref.at[pl.ds(at, size)], out_sems.at[n]))
        ins[-1].start()
        at += size
    at = 0
    for n, (j, a, b) in enumerate(chunk):
        ins[n].wait()
        for i in range((b - a) * PER_ROW):
            block = held_ref[at]
            held_ref[at] = jnp.where(flags_ref[j, a * PER_ROW + i] != 0, block, 0).astype(BF16)
            at += 1
        outs[n].start()
    for out in outs:
        out.wait()


def pack(chunk, factor, flags):
    count = sum(b - a for _, a, b in chunk) * PER_ROW
    shape = (count,) + factor.shape[2:]
    return pl.pallas_call(
        functools.partial(pack_kernel, chunk),
        in_specs=[
            pl.BlockSpec(memory_space=pltpu.SMEM),
            pl.BlockSpec(memory_space=pl.ANY),
        ],
        out_specs=pl.BlockSpec(memory_space=pl.ANY),
        out_shape=jax.ShapeDtypeStruct(shape, factor.dtype),
        scratch_shapes=[
            pltpu.VMEM(shape, factor.dtype),
            pltpu.SemaphoreType.DMA((len(chunk),)),
            pltpu.SemaphoreType.DMA((len(chunk),)),
        ],
        cost_estimate=pl.CostEstimate(
            flops=count * shape[1] * shape[2],
            bytes_accessed=4 * count * shape[1] * shape[2],
            transcendentals=0,
        ),
        name="pack",
    )(flags, factor)


def near_memory(x):
    return pltpu.with_memory_space_constraint(x, pltpu.VMEM)


def whole(shape):
    return pl.BlockSpec(memory_space=pltpu.VMEM)


def column_spec(rows, first, block):
    return pl.BlockSpec((rows, PER_ROW, block, block), lambda s: (s, first, 0, 0))


def far_rest(y, xs, packed, firsts):
    n_row, part, block = xs[0].shape[1:]
    step = n_row // FAR_STEPS
    return pl.pallas_call(
        functools.partial(far_kernel, len(xs)),
        grid=(FAR_STEPS,),
        in_specs=[whole(y.shape)]
        + [whole(x.shape) for x in xs]
        + [column_spec(step, f, block) for f in firsts],
        out_specs=whole((part, block)),
        out_shape=pltpu.VMEM((part, block), F32),
        cost_estimate=pl.CostEstimate(
            flops=2 * len(xs) * n_row * PER_ROW * part * block * block,
            bytes_accessed=2 * len(xs) * n_row * PER_ROW * block * block,
            transcendentals=0,
        ),
        name="far_rest",
    )(near_memory(y), *map(near_memory, xs), *([packed] * len(xs)))


def near_solve(xs, packed, firsts, rest, inverse, n_col):
    n_row, part, block = xs[0].shape[1:]
    steps = 1 if len(xs) == 1 else 2 * FAR_STEPS
    return pl.pallas_call(
        functools.partial(near_kernel, len(xs), steps),
        grid=(steps,),
        in_specs=[whole(x.shape) for x in xs]
        + [column_spec(n_row // steps, f, block) for f in firsts]
        + [whole(rest.shape), whole(inverse.shape)],
        out_specs=[whole((part, block)), whole((n_col, part, block))],
        out_shape=[
            pltpu.VMEM((part, block), F32),
            pltpu.VMEM((n_col, part, block), BF16),
        ],
        scratch_shapes=[pltpu.VMEM((part, block), F32)],
        cost_estimate=pl.CostEstimate(
            flops=2 * len(xs) * n_row * PER_ROW * part * block * block,
            bytes_accessed=2 * len(xs) * n_row * PER_ROW * block * block,
            transcendentals=0,
        ),
        name="near_solve",
    )(*map(near_memory, xs), *([packed] * len(xs)), near_memory(rest), near_memory(inverse))


def per_device(factor, pattern, loads, block_inverse):
    my_row = lax.axis_index("row")
    n_row = lax.axis_size("row")
    n_grp = lax.axis_size("grp")
    n_sub = lax.axis_size("sub")
    n_col = n_grp * n_sub
    scen = loads.shape[3]
    block = loads.shape[2]
    part = scen // n_row
    inverse = block_inverse[:, 0]
    loads_t = jnp.swapaxes(loads[:, 0], 1, 2)

    def forward_solve(level, resid):
        return lax.dot_general(
            resid, inverse[level], (((1,), (1,)), ((), ())), precision=HIGHEST
        )

    def backward_solve(level, resid):
        return lax.dot_general(
            resid, inverse[level], (((1,), (0,)), ((), ())), precision=HIGHEST
        )

    solved = [forward_solve(0, loads_t[0])]
    low = [solved[0].astype(BF16)]

    columns = []
    for j in range(NATIVE + 1):
        rows = slice((j + 1) * PER_ROW, LEVELS * PER_ROW)
        columns.append(factor[rows, 0, j, 0] * pattern[rows, 0, j, 0].astype(BF16)[:, None, None])

    flags = pattern[:, 0, :, 0].T
    flags_after, low[0] = lax.optimization_barrier((flags, low[0]))
    place = {}
    for number, chunk in enumerate(CHUNKS):
        packed = pack(chunk, factor[:, 0, :, 0], flags_after if number else flags)
        packed = lax.all_gather(packed, "row", axis=0)
        at = 0
        for j, a, b in chunk:
            for t in range(a, b):
                place[t, j] = packed, at
                at += 1

    def local(t, m):
        return columns[m][(t - m - 1) * PER_ROW : (t - m) * PER_ROW]

    def split(t, m):
        packed, at = place[t, m]
        return packed[:, at * PER_ROW : (at + 1) * PER_ROW]

    def local_sums(t, count):
        return sum(
            jnp.einsum("sq,apq->asp", low[m], local(t, m), preferred_element_type=F32)
            for m in range(count)
        ).astype(BF16)

    for t in range(1, NATIVE + 1):
        pieces = local_sums(t, t).reshape(n_col, part, block)
        total = jnp.sum(exchange(pieces, COL).astype(F32), axis=0).astype(BF16)
        total = exchange(spread(total, "row", n_row), "sub")
        total = total.reshape(scen, block).astype(F32)
        solved.append(forward_solve(t, loads_t[t] - total))
        low.append(solved[t].astype(BF16))

    pieces = jnp.stack(
        [local_sums(t, NATIVE + 1).reshape(n_col, part, block) for t in range(NATIVE + 1, LEVELS)],
        axis=1,
    )
    total = jnp.sum(exchange(pieces, COL).astype(F32), axis=0).astype(BF16)
    turn = [
        ((r * n_grp + g) * n_sub + k, (k * n_grp + g) * n_sub + r)
        for r in range(n_row)
        for g in range(n_grp)
        for k in range(n_sub)
    ]
    early = lax.ppermute(total, ALL, turn).astype(F32)

    def own(value):
        return lax.dynamic_slice_in_dim(value, my_row * part, part, axis=0)

    solved = [own(v) for v in solved]
    low = low + [None] * (LEVELS - NATIVE - 1)
    for t in range(NATIVE + 1, LEVELS):
        total = early[t - NATIVE - 1]
        if t > NATIVE + 1:
            sums = sum(
                jnp.einsum("sq,rapq->arsp", low[m], split(t, m), preferred_element_type=F32)
                for m in range(NATIVE + 1, t)
            )
            pieces = sums.astype(BF16).reshape(n_col, part, block)
            total = total + jnp.sum(exchange(pieces, COL).astype(F32), axis=0)
        solved.append(forward_solve(t, own(loads_t[t]) - total))
        low[t] = solved[t].astype(BF16)

    out = [None] * LEVELS
    out[LEVELS - 1] = backward_solve(LEVELS - 1, solved[LEVELS - 1])
    wide = jnp.broadcast_to(out[LEVELS - 1].astype(BF16)[None], (n_col, part, block))
    later = []
    for j in reversed(range(LEVELS - 1)):
        rest, packed = solved[j], place[j + 1, j][0]
        joined = [(t, x) for t, x in later if j == 0 and place[t, j][0] is packed]
        far = later[: len(later) - len(joined)]
        if far:
            rest = far_rest(
                rest,
                [x for _, x in far],
                place[far[0][0], j][0],
                [place[t, j][1] for t, _ in far],
            )
        if j == OUT_SPLIT - 1:
            upper, rest = lax.optimization_barrier((jnp.stack(out[j + 1 :]).astype(BF16), rest))
            upper, wide = lax.optimization_barrier((spread(upper, "row", n_row), wide))
        near = exchange(wide, COL).reshape(PER_ROW, n_row, part, block)
        joined.append((j + 1, near))
        out[j], wide = near_solve(
            [x for _, x in joined],
            packed,
            [place[t, j][1] for t, _ in joined],
            rest,
            inverse[j],
            n_col,
        )
        later.append((j + 1, near))

    lower = spread(jnp.stack(out[:OUT_SPLIT]).astype(BF16), "row", n_row)
    both = jnp.concatenate([lower, upper], axis=1)
    return jnp.transpose(both, (1, 3, 0, 2)).reshape(LEVELS, 1, block, scen).astype(F32)


def solution(mesh):
    n_col = mesh.shape["col"]
    n_row = mesh.shape["row"]
    devices = mesh.devices.reshape(n_row, n_col // SUB, SUB)
    in_specs = (
        P(None, "row", None, COL, None, None),
        P(None, "row", None, COL),
        P(None, COL, None, None),
        P(None, COL, None, None),
    )
    return jax.shard_map(
        per_device,
        mesh=Mesh(devices, ALL),
        in_specs=in_specs,
        out_specs=P(None, COL, None, None),
        check_vma=False,
    )
```

```python
import functools

import jax
import jax.numpy as jnp
from jax import lax
from jax.experimental import pallas as pl
from jax.experimental.pallas import tpu as pltpu
from jax.sharding import Mesh
from jax.sharding import PartitionSpec as P

LEVELS = 8
NATIVE = 2
FAR_STEPS = 2
OUT_SPLIT = 3
PER_ROW = 4
SUB = 8
BF16 = jnp.bfloat16
F32 = jnp.float32
HIGHEST = lax.Precision.HIGHEST
COL = ("grp", "sub")
ALL = ("row", "grp", "sub")
CHUNKS = (
    ((6, 7, 8), (5, 6, 8), (4, 5, 8), (3, 4, 8)),
    ((2, 3, 8), (1, 2, 8), (0, 7, 8)),
    ((0, 1, 7),),
)


def exchange(pieces, axis):
    return lax.all_to_all(pieces, axis, 0, 0, tiled=True)


def spread(piece, axis, count):
    return exchange(jnp.broadcast_to(piece[None], (count,) + piece.shape), axis)


def times_column(x_ref, g_ref, rows):
    x = jnp.concatenate([x_ref[a, r] for r in rows for a in range(PER_ROW)], axis=1)
    g = g_ref[...].reshape(-1, g_ref.shape[-1])
    return jnp.dot(x, g, preferred_element_type=F32)


def far_kernel(count, *refs):
    y_ref, x_refs, g_refs, out_ref = refs[0], refs[1 : count + 1], refs[count + 1 : -1], refs[-1]
    n_row = x_refs[0].shape[1]
    step = n_row // FAR_STEPS
    for s in range(FAR_STEPS):

        @pl.when(pl.program_id(0) == s)
        def _():
            rows = range(s * step, (s + 1) * step)
            got = sum(times_column(x, g, rows) for x, g in zip(x_refs, g_refs))
            out_ref[...] = (y_ref[...] if s == 0 else out_ref[...]) - got


def near_kernel(count, steps, *refs):
    x_refs, g_refs = refs[:count], refs[count : 2 * count]
    rest_ref, inverse_ref, out_ref, low_ref, acc_ref = refs[2 * count :]
    step = x_refs[0].shape[1] // steps
    for s in range(steps):

        @pl.when(pl.program_id(0) == s)
        def _():
            rows = range(s * step, (s + 1) * step)
            got = sum(times_column(x, g, rows) for x, g in zip(x_refs, g_refs))
            rest = (rest_ref[...] if s == 0 else acc_ref[...]) - got
            if s < steps - 1:
                acc_ref[...] = rest
            else:
                solved = jnp.dot(
                    rest, inverse_ref[...], precision=HIGHEST, preferred_element_type=F32
                )
                out_ref[...] = solved
                low_ref[...] = jnp.broadcast_to(solved.astype(BF16)[None], low_ref.shape)


def pack_kernel(chunk, flags_ref, factor_ref, out_ref, sems):
    copies, at = [], 0
    for n, (j, a, b) in enumerate(chunk):
        size = (b - a) * PER_ROW
        copies.append(
            pltpu.make_async_copy(
                factor_ref.at[pl.ds(a * PER_ROW, size), j], out_ref.at[pl.ds(at, size)], sems.at[n]
            )
        )
        copies[-1].start()
        at += size
    at = 0
    for copy, (j, a, b) in zip(copies, chunk):
        copy.wait()
        for i in range((b - a) * PER_ROW):
            block = out_ref[at]
            out_ref[at] = jnp.where(flags_ref[j, a * PER_ROW + i] != 0, block, 0).astype(BF16)
            at += 1


def pack(chunk, factor, flags):
    count = sum(b - a for _, a, b in chunk) * PER_ROW
    shape = (count,) + factor.shape[2:]
    return pl.pallas_call(
        functools.partial(pack_kernel, chunk),
        in_specs=[
            pl.BlockSpec(memory_space=pltpu.SMEM),
            pl.BlockSpec(memory_space=pl.ANY),
        ],
        out_specs=pl.BlockSpec(memory_space=pltpu.VMEM),
        out_shape=jax.ShapeDtypeStruct(shape, factor.dtype),
        scratch_shapes=[pltpu.SemaphoreType.DMA((len(chunk),))],
        cost_estimate=pl.CostEstimate(
            flops=count * shape[1] * shape[2],
            bytes_accessed=4 * count * shape[1] * shape[2],
            transcendentals=0,
        ),
        name="pack",
    )(flags, factor)


def near_memory(x):
    return pltpu.with_memory_space_constraint(x, pltpu.VMEM)


def whole(shape):
    return pl.BlockSpec(memory_space=pltpu.VMEM)


def column_spec(rows, first, block):
    return pl.BlockSpec((rows, PER_ROW, block, block), lambda s: (s, first, 0, 0))


def far_rest(y, xs, packed, firsts):
    n_row, part, block = xs[0].shape[1:]
    step = n_row // FAR_STEPS
    return pl.pallas_call(
        functools.partial(far_kernel, len(xs)),
        grid=(FAR_STEPS,),
        in_specs=[whole(y.shape)]
        + [whole(x.shape) for x in xs]
        + [column_spec(step, f, block) for f in firsts],
        out_specs=whole((part, block)),
        out_shape=pltpu.VMEM((part, block), F32),
        cost_estimate=pl.CostEstimate(
            flops=2 * len(xs) * n_row * PER_ROW * part * block * block,
            bytes_accessed=2 * len(xs) * n_row * PER_ROW * block * block,
            transcendentals=0,
        ),
        name="far_rest",
    )(near_memory(y), *map(near_memory, xs), *([packed] * len(xs)))


def near_solve(xs, packed, firsts, rest, inverse, n_col):
    n_row, part, block = xs[0].shape[1:]
    steps = 1 if len(xs) == 1 else FAR_STEPS
    return pl.pallas_call(
        functools.partial(near_kernel, len(xs), steps),
        grid=(steps,),
        in_specs=[whole(x.shape) for x in xs]
        + [column_spec(n_row // steps, f, block) for f in firsts]
        + [whole(rest.shape), whole(inverse.shape)],
        out_specs=[whole((part, block)), whole((n_col, part, block))],
        out_shape=[
            pltpu.VMEM((part, block), F32),
            pltpu.VMEM((n_col, part, block), BF16),
        ],
        scratch_shapes=[pltpu.VMEM((part, block), F32)],
        cost_estimate=pl.CostEstimate(
            flops=2 * len(xs) * n_row * PER_ROW * part * block * block,
            bytes_accessed=2 * len(xs) * n_row * PER_ROW * block * block,
            transcendentals=0,
        ),
        name="near_solve",
    )(*map(near_memory, xs), *([packed] * len(xs)), near_memory(rest), near_memory(inverse))


def per_device(factor, pattern, loads, block_inverse):
    my_row = lax.axis_index("row")
    n_row = lax.axis_size("row")
    n_grp = lax.axis_size("grp")
    n_sub = lax.axis_size("sub")
    n_col = n_grp * n_sub
    scen = loads.shape[3]
    block = loads.shape[2]
    part = scen // n_row
    inverse = block_inverse[:, 0]
    loads_t = jnp.swapaxes(loads[:, 0], 1, 2)

    def forward_solve(level, resid):
        return lax.dot_general(
            resid, inverse[level], (((1,), (1,)), ((), ())), precision=HIGHEST
        )

    def backward_solve(level, resid):
        return lax.dot_general(
            resid, inverse[level], (((1,), (0,)), ((), ())), precision=HIGHEST
        )

    solved = [forward_solve(0, loads_t[0])]
    low = [solved[0].astype(BF16)]

    columns = []
    for j in range(NATIVE + 1):
        rows = slice((j + 1) * PER_ROW, LEVELS * PER_ROW)
        columns.append(factor[rows, 0, j, 0] * pattern[rows, 0, j, 0].astype(BF16)[:, None, None])

    flags = pattern[:, 0, :, 0].T
    flags_after, low[0] = lax.optimization_barrier((flags, low[0]))
    place = {}
    for number, chunk in enumerate(CHUNKS):
        packed = pack(chunk, factor[:, 0, :, 0], flags_after if number else flags)
        packed = lax.all_gather(packed, "row", axis=0)
        at = 0
        for j, a, b in chunk:
            for t in range(a, b):
                place[t, j] = packed, at
                at += 1

    def local(t, m):
        return columns[m][(t - m - 1) * PER_ROW : (t - m) * PER_ROW]

    def split(t, m):
        packed, at = place[t, m]
        return packed[:, at * PER_ROW : (at + 1) * PER_ROW]

    def local_sums(t, count):
        return sum(
            jnp.einsum("sq,apq->asp", low[m], local(t, m), preferred_element_type=F32)
            for m in range(count)
        ).astype(BF16)

    for t in range(1, NATIVE + 1):
        pieces = local_sums(t, t).reshape(n_col, part, block)
        total = jnp.sum(exchange(pieces, COL).astype(F32), axis=0).astype(BF16)
        total = exchange(spread(total, "row", n_row), "sub")
        total = total.reshape(scen, block).astype(F32)
        solved.append(forward_solve(t, loads_t[t] - total))
        low.append(solved[t].astype(BF16))

    pieces = jnp.stack(
        [local_sums(t, NATIVE + 1).reshape(n_col, part, block) for t in range(NATIVE + 1, LEVELS)],
        axis=1,
    )
    total = jnp.sum(exchange(pieces, COL).astype(F32), axis=0).astype(BF16)
    turn = [
        ((r * n_grp + g) * n_sub + k, (k * n_grp + g) * n_sub + r)
        for r in range(n_row)
        for g in range(n_grp)
        for k in range(n_sub)
    ]
    early = lax.ppermute(total, ALL, turn).astype(F32)

    def own(value):
        return lax.dynamic_slice_in_dim(value, my_row * part, part, axis=0)

    solved = [own(v) for v in solved]
    low = low + [None] * (LEVELS - NATIVE - 1)
    for t in range(NATIVE + 1, LEVELS):
        total = early[t - NATIVE - 1]
        if t > NATIVE + 1:
            sums = sum(
                jnp.einsum("sq,rapq->arsp", low[m], split(t, m), preferred_element_type=F32)
                for m in range(NATIVE + 1, t)
            )
            pieces = sums.astype(BF16).reshape(n_col, part, block)
            total = total + jnp.sum(exchange(pieces, COL).astype(F32), axis=0)
        solved.append(forward_solve(t, own(loads_t[t]) - total))
        low[t] = solved[t].astype(BF16)

    out = [None] * LEVELS
    out[LEVELS - 1] = backward_solve(LEVELS - 1, solved[LEVELS - 1])
    wide = jnp.broadcast_to(out[LEVELS - 1].astype(BF16)[None], (n_col, part, block))
    later = []
    for j in reversed(range(LEVELS - 1)):
        rest, packed = solved[j], place[j + 1, j][0]
        joined = [(t, x) for t, x in later if j == 0 and place[t, j][0] is packed]
        far = later[: len(later) - len(joined)]
        if far:
            rest = far_rest(
                rest,
                [x for _, x in far],
                place[far[0][0], j][0],
                [place[t, j][1] for t, _ in far],
            )
        if j == OUT_SPLIT - 1:
            upper = spread(jnp.stack(out[j + 1 :]).astype(BF16), "row", n_row)
            upper, wide = lax.optimization_barrier((upper, wide))
        near = exchange(wide, COL).reshape(PER_ROW, n_row, part, block)
        joined.append((j + 1, near))
        out[j], wide = near_solve(
            [x for _, x in joined],
            packed,
            [place[t, j][1] for t, _ in joined],
            rest,
            inverse[j],
            n_col,
        )
        later.append((j + 1, near))

    lower = spread(jnp.stack(out[:OUT_SPLIT]).astype(BF16), "row", n_row)
    both = jnp.concatenate([lower, upper], axis=1)
    return jnp.transpose(both, (1, 3, 0, 2)).reshape(LEVELS, 1, block, scen).astype(F32)


def solution(mesh):
    n_col = mesh.shape["col"]
    n_row = mesh.shape["row"]
    devices = mesh.devices.reshape(n_row, n_col // SUB, SUB)
    in_specs = (
        P(None, "row", None, COL, None, None),
        P(None, "row", None, COL),
        P(None, COL, None, None),
        P(None, COL, None, None),
    )
    return jax.shard_map(
        per_device,
        mesh=Mesh(devices, ALL),
        in_specs=in_specs,
        out_specs=P(None, COL, None, None),
        check_vma=False,
    )
```
